32 devices in a mesh: scen: 2 (over x), node: 16 (over z, y, core).
Axes of the slice: x: 2, y: 2, z: 4, core: 2. Of those that a mesh axis runs over, the one named last changes fastest.
Arguments:
- hidden_state: bfloat16 [65536, 128], P(('scen', 'node')), parts along dimension 0, may hold values from -6 to 6
- conv_cache: bfloat16 [3, 65536, 128], P(None, ('scen', 'node')), parts along dimension 1, may hold values from -6 to 6
- conv_weight: bfloat16 [3, 256, 512], replicated, may hold values from -0.375 to 0.375
- conv_bias: float32 [3, 512], replicated, may hold values from -3 to 3
- mix_weight: bfloat16 [3, 768, 128], replicated, may hold values from -0.21875 to 0.21875
- skip_weight: bfloat16 [3, 256, 256], replicated, may hold values from -0.375 to 0.375
- block_values: bfloat16 [752, 128, 128], P('node'), may hold values from -0.3125 to 0.3125
- block_target: int32 [752], P('node'), may hold values from 0 to 15, as said below
- block_owner: int32 [752], P('node'), may hold values from 0 to 15, as said below
- block_slot: int32 [752], P('node'), may hold values from 0 to 15, as said below
- send_tiles: int32 [16, 16, 2], P('node'), may hold values from 0 to 15
- send_count: int32 [16, 16], P('node'), may hold values from 0 to 2, as said below
Outputs:
- next_state: bfloat16 [65536, 128], P(('scen', 'node')), parts along dimension 0
- skip_total: bfloat16 [65536, 256], P(('scen', 'node')), parts along dimension 0
The draws below stay inside these ranges and needn't reach their ends.
There are 2 independent parts, one for each index of `scen`. The reference program is written for one: setup_inputs(seed, part) draws one part's arguments, and reference() takes and returns one part's arrays. A program takes and returns all parts, laid end to end along the dimension named above; an argument that names none is the same for every part. Nothing has to cross between parts.
Inputs may be any that keep to these rules, and one draw needn't show every extreme that they name: `block_target`: each device's blocks target its own tiles; every tile has one block whose source is itself and one whose source is another tile of the same device. `block_owner`: each device has 32 blocks owned by itself and 15 owned by other devices. `block_slot`: for a remote owner o, the slot is below send_count[o, device], and each such slot is used by exactly one block of the device. `send_count`: zero from a device to itself; the counts into one device sum to 15; some pair reaches 2 in every draw.
All inputs are finite; a program needn't handle non-finite values.
Results may differ from the reference program's by a relative error of at most 0.01.
Values may be sent and summed in bfloat16 or wider, within the bound.
No kernel may reach another device: no remote copies, remote signals or barrier semaphores. Data moves between devices by JAX's collectives and lax.ppermute only.
A program may use at most 128 MiB of HBM per device.

```python
import jax
import jax.numpy as jnp
from jax import lax

RES = 128
GATE = 256
SKIP = 256
TILE = 128
TILES_DEV = 16
CAP = 2
LAYERS = 3
PEERS = 16
REMOTE = 15
BLK_DEV = 47
BLOCKS = 752
TILES = 256
NODES = 32768


def build_graph(key):
    base_key = jax.random.fold_in(key, 5)

    def one_device(device):
        device_key = jax.random.fold_in(base_key, device)
        keys = jax.random.split(device_key, 5)
        candidates = (PEERS - 1) * CAP
        ranking = jax.random.permutation(keys[0], candidates).astype(jnp.int32)
        forced = jax.random.randint(keys[1], (), 0, PEERS - 1)
        cand_index = jnp.arange(candidates, dtype=jnp.int32)
        priority = jnp.where(cand_index // CAP == forced, cand_index % CAP - CAP, ranking)
        order = jnp.argsort(priority, stable=True).astype(jnp.int32)
        chosen = order[:REMOTE]
        chosen_peer = chosen // CAP
        positions = jnp.arange(REMOTE, dtype=jnp.int32)
        earlier = jnp.logical_and(chosen_peer[None, :] == chosen_peer[:, None], positions[None, :] < positions[:, None])
        remote_slot = jnp.sum(earlier.astype(jnp.int32), axis=1)
        remote_owner = (device + 1 + chosen_peer) % PEERS
        peer_index = jnp.arange(PEERS - 1, dtype=jnp.int32)
        per_peer = jnp.sum((chosen_peer[:, None] == peer_index[None, :]).astype(jnp.int32), axis=0)
        count_row = jnp.zeros((PEERS,), jnp.int32).at[(device + 1 + peer_index) % PEERS].set(per_peer)
        remote_target = jax.random.randint(keys[2], (REMOTE,), 0, TILES_DEV)
        tile_index = jnp.arange(TILES_DEV, dtype=jnp.int32)
        offsets = jax.random.randint(keys[3], (TILES_DEV,), 1, TILES_DEV)
        local_source = (tile_index + offsets) % TILES_DEV
        owner_self = jnp.full((TILES_DEV,), device, jnp.int32)
        targets = jnp.concatenate([tile_index, tile_index, remote_target])
        owners = jnp.concatenate([owner_self, owner_self, remote_owner])
        slots = jnp.concatenate([tile_index, local_source, remote_slot])
        shuffle = jax.random.permutation(keys[4], BLK_DEV)
        return (targets[shuffle], owners[shuffle], slots[shuffle], count_row)
    targets, owners, slots, counts = jax.vmap(one_device)(jnp.arange(PEERS, dtype=jnp.int32))
    return (targets.reshape(-1).astype(jnp.int32), owners.reshape(-1).astype(jnp.int32), slots.reshape(-1).astype(jnp.int32), jnp.transpose(counts).astype(jnp.int32))


def draw_block_target(key, part):
    return build_graph(key)[0]


def draw_block_owner(key, part):
    return build_graph(key)[1]


def draw_block_slot(key, part):
    return build_graph(key)[2]


def draw_send_count(key, part):
    return build_graph(key)[3]


def draw_send_tiles(key, part):
    keys = jax.random.split(jax.random.fold_in(key, 11), 2)
    total = PEERS * PEERS * CAP
    values = jax.random.randint(keys[0], (total,), 0, TILES_DEV)
    chosen_spot = jax.random.randint(keys[1], (), 0, total)
    values = jnp.where(jnp.arange(total, dtype=jnp.int32) == chosen_spot, TILES_DEV - 1, values)
    return values.reshape(PEERS, PEERS, CAP).astype(jnp.int32)


def block_levels(stream_key, shape, pieces, smallest, top_value):
    def one(axis_at, parts):
        heights = jax.random.uniform(jax.random.fold_in(jax.random.fold_in(stream_key, 6), axis_at), (parts,), jnp.float32, smallest / len(pieces), top_value / len(pieces))
        return jnp.repeat(jnp.exp(heights), shape[axis_at] // parts).reshape((-1,) + (1,) * (len(shape) - axis_at - 1))

    loudness = one(*pieces[0])
    for cut in pieces[1:]:
        loudness = loudness * one(*cut)
    return loudness


def bell_draw(rng, extent, width, reach, cuts=(), kind=jnp.bfloat16):
    factor_of = block_levels(rng, extent, cuts, -0.22, 0.18) if cuts else 1.0
    drawn = jax.random.normal(rng, extent, jnp.float32) * width * factor_of
    return jnp.minimum(jnp.maximum(drawn, -reach), reach).astype(kind)


def setup_inputs(seed: int = 0, part: int = 0) -> dict:
    arg_keys = jax.random.split(jax.random.key(seed), 13)
    own_keys = jax.random.split(jax.random.fold_in(arg_keys[12], part), 13)
    hidden_state = bell_draw(own_keys[0], (NODES, RES), 1.0, 6.0, ((0, 16),))
    conv_cache = bell_draw(own_keys[1], (LAYERS, NODES, RES), 1.0, 6.0, ((1, 16),))
    conv_weight = bell_draw(arg_keys[2], (LAYERS, 2 * RES, 2 * GATE), (2 * RES) ** -0.5, 0.375)
    conv_bias = bell_draw(arg_keys[3], (LAYERS, 2 * GATE), 0.5, 3.0, (), jnp.float32)
    mix_weight = bell_draw(arg_keys[4], (LAYERS, 3 * GATE, RES), (3 * GATE) ** -0.5, 0.21875)
    skip_weight = bell_draw(arg_keys[5], (LAYERS, GATE, SKIP), GATE ** -0.5, 0.375)
    block_values = bell_draw(arg_keys[6], (BLOCKS, TILE, TILE), (BLK_DEV * TILE // TILES_DEV) ** -0.5, 0.3125, ((0, 16),))
    block_target = draw_block_target(jax.random.fold_in(arg_keys[12], 71), part)
    block_owner = draw_block_owner(jax.random.fold_in(arg_keys[12], 71), part)
    block_slot = draw_block_slot(jax.random.fold_in(arg_keys[12], 71), part)
    send_tiles = draw_send_tiles(jax.random.fold_in(arg_keys[12], 71), part)
    send_count = draw_send_count(jax.random.fold_in(arg_keys[12], 71), part)
    return dict(hidden_state=hidden_state, conv_cache=conv_cache, conv_weight=conv_weight, conv_bias=conv_bias, mix_weight=mix_weight, skip_weight=skip_weight, block_values=block_values, block_target=block_target, block_owner=block_owner, block_slot=block_slot, send_tiles=send_tiles, send_count=send_count)


def build_sources(block_target, block_owner, block_slot, send_tiles, send_count):
    device_of = jnp.arange(BLOCKS, dtype=jnp.int32) // BLK_DEV
    clipped = jnp.minimum(block_slot, CAP - 1)
    remote_tile = send_tiles[block_owner, device_of, clipped]
    is_self = block_owner == device_of
    source = jnp.where(is_self, device_of * TILES_DEV + block_slot, block_owner * TILES_DEV + remote_tile)
    valid = jnp.logical_or(is_self, block_slot < send_count[block_owner, device_of])
    return source.astype(jnp.int32), valid.astype(jnp.float32)


def diffuse(field, block_values, source, valid, block_target):
    tiled = field.reshape(TILES, TILE, field.shape[1])

    def per_device(packed):
        values, src, live, local_target = packed
        picked = tiled[src].astype(jnp.float32) * live[:, None, None]
        product = jnp.einsum("bij,bjc->bic", values.astype(jnp.float32), picked)
        return jax.ops.segment_sum(product, local_target, num_segments=TILES_DEV)

    result = lax.map(per_device, (block_values.reshape(PEERS, BLK_DEV, TILE, TILE), source.reshape(PEERS, BLK_DEV), valid.reshape(PEERS, BLK_DEV), block_target.reshape(PEERS, BLK_DEV)))
    return result.reshape(NODES, field.shape[1])


def reference(hidden_state, conv_cache, conv_weight, conv_bias, mix_weight, skip_weight, block_values, block_target, block_owner, block_slot, send_tiles, send_count):
    source, valid = build_sources(block_target, block_owner, block_slot, send_tiles, send_count)
    current = hidden_state
    skip_sum = jnp.zeros((NODES, SKIP), jnp.float32)
    for layer_index in range(LAYERS):
        weight_now = conv_weight[layer_index]
        preact = jnp.dot(conv_cache[layer_index], weight_now[:RES], preferred_element_type=jnp.float32)
        preact = preact + jnp.dot(current, weight_now[RES:], preferred_element_type=jnp.float32)
        preact = preact + conv_bias[layer_index]
        gated_out = (jnp.tanh(preact[:, :GATE]) * jax.nn.sigmoid(preact[:, GATE:])).astype(jnp.bfloat16)
        hop_one = diffuse(gated_out, block_values, source, valid, block_target).astype(jnp.bfloat16)
        hop_two = diffuse(hop_one, block_values, source, valid, block_target).astype(jnp.bfloat16)
        mixing = mix_weight[layer_index]
        mixed = jnp.dot(gated_out, mixing[:GATE], preferred_element_type=jnp.float32)
        mixed = mixed + jnp.dot(hop_one, mixing[GATE:2 * GATE], preferred_element_type=jnp.float32)
        mixed = mixed + jnp.dot(hop_two, mixing[2 * GATE:], preferred_element_type=jnp.float32)
        skip_sum = skip_sum + jnp.dot(gated_out, skip_weight[layer_index], preferred_element_type=jnp.float32)
        current = (current.astype(jnp.float32) + mixed).astype(jnp.bfloat16)
    return current, skip_sum.astype(jnp.bfloat16)
```

```python
import functools

import jax
import jax.numpy as jnp
from jax import lax
from jax.experimental import pallas as pl
from jax.experimental.pallas import tpu as pltpu
from jax.sharding import PartitionSpec as P

TILE = 128
CAP = 2
F32 = jnp.float32
BF16 = jnp.bfloat16
VMEM = pl.BlockSpec(memory_space=pltpu.VMEM)
SMEM = pl.BlockSpec(memory_space=pltpu.SMEM)
LIMIT = 48 << 20


def dot(a, b):
    return jnp.dot(a, b, preferred_element_type=F32)


def call(kernel, name, ins, outs, in_specs, out_specs, flops, scratch=(), alias=None):
    moved = sum(x.size * x.dtype.itemsize for x in ins) + sum(
        o.size * o.dtype.itemsize for o in outs
    )
    return pl.pallas_call(
        kernel,
        name=name,
        out_shape=tuple(outs),
        in_specs=in_specs,
        out_specs=tuple(out_specs),
        scratch_shapes=scratch,
        input_output_aliases=alias or {},
        compiler_params=pltpu.CompilerParams(vmem_limit_bytes=LIMIT),
        cost_estimate=pl.CostEstimate(flops=flops, bytes_accessed=moved, transcendentals=0),
    )(*ins)


def shape(dims, dtype):
    return jax.ShapeDtypeStruct(dims, dtype)


def fill_send(routing, field, send):
    for place in range(send.shape[0]):
        tile = routing[place]
        send[place] = field[pl.ds(pl.multiple_of(tile * TILE, TILE), TILE), :]


def add_remote(table, blocks, far, total):
    remote = blocks.shape[0]
    for j in range(remote):
        rows = pl.ds(pl.multiple_of(table[0, j] * TILE, TILE), TILE)
        total[rows, :] += dot(blocks[j], far[table[1, j]])


def convolve(past, state, weight, bias, mix, gated, second, gate):
    rows = state.shape[0]
    chunk = 512
    part = 128

    def body(i, carry):
        for k in range(chunk // part):
            at = pl.ds(pl.multiple_of(i * chunk + k * part, part), part)
            both = jnp.concatenate([past[at, :], state[at, :]], axis=1)
            pre = dot(both, weight[...]) + bias[...]
            value = jnp.tanh(pre[:, :gate]) * (0.5 * jnp.tanh(0.5 * pre[:, gate:]) + 0.5)
            value = value.astype(BF16)
            gated[at, :] = value
            second[at, :] = dot(value, mix[...]).astype(BF16)
        return carry

    lax.fori_loop(0, rows // chunk, body, 0)


def first_kernel(routing, state, past, weight, bias, mix, gated, second, send, *, gate):
    convolve(past, state, weight, bias, mix, gated, second, gate)
    fill_send(routing, second, send)


def next_kernel(
    routing, table, blocks, far, total_in, past, weight, bias, mix,
    state, gated, second, send, total, *, gate,
):
    total[...] = total_in[...]
    add_remote(table, blocks, far, total)
    state[...] = total[...].astype(BF16)
    convolve(past, state, weight, bias, mix, gated, second, gate)
    fill_send(routing, second, send)


def hop_kernel(routing, table, blocks, far, total_in, field, send, total):
    total[...] = total_in[...]
    add_remote(table, blocks, far, total)
    field[...] = total[...].astype(BF16)
    fill_send(routing, field, send)


def last_kernel(table, blocks, far, total_in, state, total):
    total[...] = total_in[...]
    add_remote(table, blocks, far, total)
    state[...] = total[...].astype(BF16)


def build_kernel(place, target, owner, slot, values, table, local, remote_blocks, *, tiles):
    me = place[0]

    def body(b, seen):
        t, o, s = target[b], owner[b], slot[b]
        mine = o == me

        @pl.when(mine)
        def _():
            row = jnp.where(s == t, 0, 1)
            local[row, t] = b
            local[row + 2, t] = s

        @pl.when(jnp.logical_not(mine))
        def _():
            table[0, seen] = t
            table[1, seen] = o * CAP + s
            remote_blocks[seen] = values[b]

        return seen + jnp.where(mine, 0, 1)

    lax.fori_loop(0, target.shape[0], body, jnp.int32(0))


def local_sum(local, values, field, t):
    other = field[pl.ds(pl.multiple_of(local[3, t] * TILE, TILE), TILE), :]
    own = field[pl.ds(t * TILE, TILE), :]
    block = jnp.concatenate([values[local[0, t]], values[local[1, t]]], axis=1)
    return dot(block, jnp.concatenate([own, other], axis=0))


def under_first_kernel(
    local, values, gated, second, wide, skip_in, total, base, skip, *, res
):
    for t in range(gated.shape[0] // TILE):
        at = pl.ds(t * TILE, TILE)
        out = dot(gated[at, :], wide[...])
        total[at, :] = out[:, :res] + local_sum(local, values, second, t)
        base[at, :] = out[:, res : 2 * res]
        if skip_in is None:
            skip[at, :] = out[:, 2 * res :].astype(skip.dtype)
        else:
            skip[at, :] = (skip_in[at, :] + out[:, 2 * res :]).astype(skip.dtype)


def under_second_kernel(local, values, field, base, state, total):
    for t in range(field.shape[0] // TILE):
        at = pl.ds(t * TILE, TILE)
        total[at, :] = (
            state[at, :].astype(F32) + base[at, :] + local_sum(local, values, field, t)
        )


def local(
    hidden_state,
    conv_cache,
    conv_weight,
    conv_bias,
    mix_weight,
    skip_weight,
    block_values,
    block_target,
    block_owner,
    block_slot,
    send_tiles,
    send_count,
):
    rows, res = hidden_state.shape
    layers = conv_cache.shape[0]
    gate, skips = skip_weight.shape[1:]
    tiles = rows // TILE
    peers = send_tiles.shape[1]
    slots = peers * CAP
    blocks = block_values.shape[0]
    remote = blocks - 2 * tiles
    place = lax.axis_index("node").astype(jnp.int32)[None]
    routing = send_tiles.reshape(slots)

    table, local_table, remote_blocks = call(
        functools.partial(build_kernel, tiles=tiles),
        "sort_blocks",
        (place, block_target, block_owner, block_slot, block_values),
        (
            shape((2, remote), jnp.int32),
            shape((4, tiles), jnp.int32),
            shape((remote, TILE, TILE), BF16),
        ),
        [SMEM] * 4 + [VMEM],
        [SMEM, SMEM, VMEM],
        blocks * 1000,
    )

    def exchange(send):
        got = lax.all_to_all(
            send.reshape(peers, CAP, TILE, res), "node", split_axis=0, concat_axis=0, tiled=True
        )
        return got.reshape(slots, TILE, res)

    conv_flops = 2 * rows * (2 * res * 2 * gate + gate * res)
    hop_flops = 2 * remote * TILE * TILE * res
    conv_outs = (
        shape((rows, gate), BF16),
        shape((rows, res), BF16),
        shape((slots, TILE, res), BF16),
    )
    state = hidden_state
    skip = None
    total = far = None
    for layer in range(layers):
        mixing = mix_weight[layer]
        weight, bias = conv_weight[layer], conv_bias[layer][None, :]
        wide = jnp.concatenate(
            [mixing[gate : 2 * gate], mixing[:gate], skip_weight[layer]], axis=1
        )
        deep = mixing[2 * gate :]
        if layer == 0:
            gated, second, send = call(
                functools.partial(first_kernel, gate=gate),
                "conv_first",
                (routing, state, conv_cache[layer], weight, bias, deep),
                conv_outs,
                [SMEM] + [VMEM] * 5,
                [VMEM] * 3,
                conv_flops,
            )
        else:
            state, gated, second, send = call(
                functools.partial(next_kernel, gate=gate),
                "conv_next",
                (routing, table, remote_blocks, far, total, conv_cache[layer], weight, bias, deep),
                (shape((rows, res), BF16),) + conv_outs,
                [SMEM] * 2 + [VMEM] * 7,
                [VMEM] * 4,
                conv_flops + hop_flops,
                [pltpu.VMEM((rows, res), F32)],
            )
        far = exchange(send)
        last = layer == layers - 1
        first_ins = (local_table, block_values, gated, second, wide)
        kernel = functools.partial(under_first_kernel, res=res)
        if layer == 0:
            ins = first_ins

            def body(l, v, g, s, w, t, b, k):
                under_first_kernel(l, v, g, s, w, None, t, b, k, res=res)

        else:
            ins = first_ins + (skip,)
            body = kernel
        total, base, skip = call(
            body,
            "under_first",
            ins,
            (
                shape((rows, res), F32),
                shape((rows, res), F32),
                shape((rows, skips), BF16 if last else F32),
            ),
            [SMEM] + [VMEM] * (len(ins) - 1),
            [VMEM] * 3,
            2 * rows * gate * (2 * res + skips) + 4 * rows * TILE * res,
        )
        field, send = call(
            hop_kernel,
            "hop",
            (routing, table, remote_blocks, far, total),
            (shape((rows, res), BF16), shape((slots, TILE, res), BF16)),
            [SMEM] * 2 + [VMEM] * 3,
            [VMEM] * 2,
            hop_flops,
            [pltpu.VMEM((rows, res), F32)],
        )
        far = exchange(send)
        (total,) = call(
            under_second_kernel,
            "under_second",
            (local_table, block_values, field, base, state),
            (shape((rows, res), F32),),
            [SMEM] + [VMEM] * 4,
            [VMEM],
            4 * rows * TILE * res,
        )
    (state,) = call(
        last_kernel,
        "last",
        (table, remote_blocks, far, total),
        (shape((rows, res), BF16),),
        [SMEM] + [VMEM] * 3,
        [VMEM],
        hop_flops,
        [pltpu.VMEM((rows, res), F32)],
    )
    return state, skip


def solution(mesh):
    placed = (
        P(("scen", "node"), None),
        P(None, ("scen", "node"), None),
        P(),
        P(),
        P(),
        P(),
        P("node", None, None),
        P("node"),
        P("node"),
        P("node"),
        P("node", None, None),
        P("node", None),
    )
    return jax.shard_map(
        local,
        mesh=mesh,
        in_specs=placed,
        out_specs=(P(("scen", "node"), None), P(("scen", "node"), None)),
        check_vma=False,
    )
```

```python
import functools

import jax
import jax.numpy as jnp
from jax import lax
from jax.experimental import pallas as pl
from jax.experimental.pallas import tpu as pltpu
from jax.sharding import PartitionSpec as P

TILE = 128
CAP = 2
F32 = jnp.float32
BF16 = jnp.bfloat16
VMEM = pl.BlockSpec(memory_space=pltpu.VMEM)
SMEM = pl.BlockSpec(memory_space=pltpu.SMEM)
HBM = pl.BlockSpec(memory_space=pltpu.HBM)
LIMIT = 60 << 20


def dot(a, b):
    return jnp.dot(a, b, preferred_element_type=F32)


def call(kernel, name, ins, outs, in_specs, out_specs, flops, scratch=(), alias=None):
    moved = sum(x.size * x.dtype.itemsize for x in ins) + sum(
        o.size * o.dtype.itemsize for o in outs
    )
    return pl.pallas_call(
        kernel,
        name=name,
        out_shape=tuple(outs),
        in_specs=in_specs,
        out_specs=tuple(out_specs),
        scratch_shapes=scratch,
        input_output_aliases=alias or {},
        compiler_params=pltpu.CompilerParams(vmem_limit_bytes=LIMIT),
        cost_estimate=pl.CostEstimate(flops=flops, bytes_accessed=moved, transcendentals=0),
    )(*ins)


def shape(dims, dtype):
    return jax.ShapeDtypeStruct(dims, dtype)


def start(source, target, sem):
    copy = pltpu.make_async_copy(source, target, sem)
    copy.start()
    return copy


def start_send(routing, field, send, sem):
    for place in range(send.shape[0]):
        rows = pl.ds(pl.multiple_of(routing[place] * TILE, TILE), TILE)
        start(field.at[rows, :], send.at[place], sem)
    return pltpu.make_async_copy(send, send, sem)


def add_remote(table, blocks, far, total):
    for j in range(blocks.shape[0]):
        rows = pl.ds(pl.multiple_of(table[0, j] * TILE, TILE), TILE)
        total[rows, :] += dot(blocks[j], far[table[1, j]])


def convolve(past, state, weight, bias, gated):
    gate = gated.shape[1]
    part = 512
    for i in range(state.shape[0] // part):
        at = pl.ds(i * part, part)
        both = jnp.concatenate([past[at, :], state[at, :]], axis=1)
        pre = dot(both, weight[...]) + bias[...]
        value = jnp.tanh(pre[:, :gate]) * (0.5 * jnp.tanh(0.5 * pre[:, gate:]) + 0.5)
        gated[at, :] = value.astype(BF16)


def conv_loads(layer, past_all, weight_all, bias_all, mix_all, past, weight, bias, mix, sems):
    depth = mix.shape[0]
    return [
        start(weight_all.at[layer], weight, sems.at[0]),
        start(past_all.at[layer], past, sems.at[1]),
        start(bias_all.at[pl.ds(layer, 1), :], bias, sems.at[2]),
        start(mix_all.at[layer, pl.ds(2 * depth, depth), :], mix, sems.at[3]),
    ]


def conv_finish(routing, mix, gated, second, gated_out, second_out, send, sems):
    second[...] = dot(gated[...], mix[...]).astype(BF16)
    copies = [
        start_send(routing, second, send, sems.at[4]),
        start(gated, gated_out, sems.at[5]),
        start(second, second_out, sems.at[6]),
    ]
    for copy in copies:
        copy.wait()


def first_kernel(
    routing, state_in, past_all, weight_all, bias_all, mix_all,
    gated_out, second_out, send,
    past, weight, bias, mix, gated, second, state, sems, *, layer,
):
    loads = conv_loads(layer, past_all, weight_all, bias_all, mix_all, past, weight, bias, mix, sems)
    loads.append(start(state_in, state, sems.at[7]))
    for copy in loads:
        copy.wait()
    convolve(past, state, weight, bias, gated)
    conv_finish(routing, mix, gated, second, gated_out, second_out, send, sems)


def next_kernel(
    routing, table, blocks, far, total_in, past_all, weight_all, bias_all, mix_all,
    gated_out, second_out, send, state_out,
    past, weight, bias, mix, gated, second, state, total, sems, *, layer,
):
    first = start(total_in, total, sems.at[7])
    loads = conv_loads(layer, past_all, weight_all, bias_all, mix_all, past, weight, bias, mix, sems)
    first.wait()
    add_remote(table, blocks, far, total)
    state[...] = total[...].astype(BF16)
    for copy in loads:
        copy.wait()
    convolve(past, state, weight, bias, gated)
    last = start(state, state_out, sems.at[7])
    conv_finish(routing, mix, gated, second, gated_out, second_out, send, sems)
    last.wait()


def hop_kernel(routing, table, blocks, far, total_in, field_out, send, field, total, sems):
    start(total_in, total, sems.at[0]).wait()
    add_remote(table, blocks, far, total)
    field[...] = total[...].astype(BF16)
    copies = [start_send(routing, field, send, sems.at[1]), start(field, field_out, sems.at[2])]
    for copy in copies:
        copy.wait()


def last_kernel(table, blocks, far, total_in, state_out, state, total, sems):
    start(total_in, total, sems.at[0]).wait()
    add_remote(table, blocks, far, total)
    state[...] = total[...].astype(BF16)
    start(state, state_out, sems.at[1]).wait()


def build_kernel(place, target, owner, slot, values, table, local, remote_blocks, *, tiles):
    me = place[0]

    def body(b, seen):
        t, o, s = target[b], owner[b], slot[b]
        mine = o == me

        @pl.when(mine)
        def _():
            row = jnp.where(s == t, 0, 1)
            local[row, t] = b
            local[row + 2, t] = s

        @pl.when(jnp.logical_not(mine))
        def _():
            table[0, seen] = t
            table[1, seen] = o * CAP + s
            remote_blocks[seen] = values[b]

        return seen + jnp.where(mine, 0, 1)

    lax.fori_loop(0, target.shape[0], body, jnp.int32(0))


def local_sum(local, values, field, t):
    other = field[pl.ds(pl.multiple_of(local[3, t] * TILE, TILE), TILE), :]
    own = field[pl.ds(t * TILE, TILE), :]
    block = jnp.concatenate([values[local[0, t]], values[local[1, t]]], axis=1)
    return dot(block, jnp.concatenate([own, other], axis=0))


def under_first_kernel(
    local, values, gated, second, mix_all, skip_all, *rest, res, layer
):
    skip_in = rest[0] if layer else None
    total, base, skip, wide, sems = rest[1 if layer else 0 :]
    gate = gated.shape[1]
    loads = [
        start(mix_all.at[layer, pl.ds(gate, gate), :], wide.at[:, pl.ds(0, res)], sems.at[0]),
        start(mix_all.at[layer, pl.ds(0, gate), :], wide.at[:, pl.ds(res, res)], sems.at[1]),
        start(skip_all.at[layer], wide.at[:, pl.ds(2 * res, skip.shape[1])], sems.at[2]),
    ]
    for copy in loads:
        copy.wait()
    for t in range(gated.shape[0] // TILE):
        at = pl.ds(t * TILE, TILE)
        out = dot(gated[at, :], wide[...])
        total[at, :] = out[:, :res] + local_sum(local, values, second, t)
        base[at, :] = out[:, res : 2 * res]
        gain = out[:, 2 * res :]
        if layer:
            gain = gain + skip_in[at, :]
        skip[at, :] = gain.astype(skip.dtype)


def under_second_kernel(local, values, field, base, state, total):
    for t in range(field.shape[0] // TILE):
        at = pl.ds(t * TILE, TILE)
        total[at, :] = (
            state[at, :].astype(F32) + base[at, :] + local_sum(local, values, field, t)
        )


def local(
    hidden_state,
    conv_cache,
    conv_weight,
    conv_bias,
    mix_weight,
    skip_weight,
    block_values,
    block_target,
    block_owner,
    block_slot,
    send_tiles,
    send_count,
):
    rows, res = hidden_state.shape
    layers = conv_cache.shape[0]
    gate, skips = skip_weight.shape[1:]
    tiles = rows // TILE
    peers = send_tiles.shape[1]
    slots = peers * CAP
    blocks = block_values.shape[0]
    remote = blocks - 2 * tiles
    place = lax.axis_index("node").astype(jnp.int32)[None]
    routing = send_tiles.reshape(slots)

    table, local_table, remote_blocks = call(
        functools.partial(build_kernel, tiles=tiles),
        "sort_blocks",
        (place, block_target, block_owner, block_slot, block_values),
        (
            shape((2, remote), jnp.int32),
            shape((4, tiles), jnp.int32),
            shape((remote, TILE, TILE), BF16),
        ),
        [SMEM] * 4 + [VMEM],
        [SMEM, SMEM, VMEM],
        blocks * 1000,
    )

    def exchange(send):
        got = lax.all_to_all(
            send.reshape(peers, CAP, TILE, res), "node", split_axis=0, concat_axis=0, tiled=True
        )
        return got.reshape(slots, TILE, res)

    conv_flops = 2 * rows * (2 * res * 2 * gate + gate * res)
    hop_flops = 2 * remote * TILE * TILE * res
    conv_outs = (
        shape((rows, gate), BF16),
        shape((rows, res), BF16),
        shape((slots, TILE, res), BF16),
    )
    conv_scratch = [
        pltpu.VMEM((rows, res), BF16),
        pltpu.VMEM((2 * res, 2 * gate), BF16),
        pltpu.VMEM((1, 2 * gate), F32),
        pltpu.VMEM((gate, res), BF16),
        pltpu.VMEM((rows, gate), BF16),
        pltpu.VMEM((rows, res), BF16),
        pltpu.VMEM((rows, res), BF16),
    ]
    wide_field = pltpu.VMEM((rows, res), F32)
    thin_field = pltpu.VMEM((rows, res), BF16)
    weights = (conv_cache, conv_weight, conv_bias, mix_weight)
    state = hidden_state
    skip = None
    total = far = None
    for layer in range(layers):
        if layer == 0:
            gated, second, send = call(
                functools.partial(first_kernel, layer=layer),
                "conv_first",
                (routing, state) + weights,
                conv_outs,
                [SMEM] + [HBM] * 5,
                [HBM] * 3,
                conv_flops,
                conv_scratch + [pltpu.SemaphoreType.DMA((8,))],
            )
        else:
            gated, second, send, state = call(
                functools.partial(next_kernel, layer=layer),
                "conv_next",
                (routing, table, remote_blocks, far, total) + weights,
                conv_outs + (shape((rows, res), BF16),),
                [SMEM] * 2 + [VMEM] * 2 + [HBM] * 5,
                [HBM] * 4,
                conv_flops + hop_flops,
                conv_scratch + [wide_field, pltpu.SemaphoreType.DMA((8,))],
            )
        far = exchange(send)
        last = layer == layers - 1
        ins = (local_table, block_values, gated, second, mix_weight, skip_weight)
        if layer:
            ins += (skip,)
        total, base, skip = call(
            functools.partial(under_first_kernel, res=res, layer=layer),
            "under_first",
            ins,
            (
                shape((rows, res), F32),
                shape((rows, res), F32),
                shape((rows, skips), BF16 if last else F32),
            ),
            [SMEM] + [VMEM] * 3 + [HBM] * 2 + [VMEM] * (len(ins) - 6),
            [VMEM] * 3,
            2 * rows * gate * (2 * res + skips) + 4 * rows * TILE * res,
            [pltpu.VMEM((gate, 2 * res + skips), BF16), pltpu.SemaphoreType.DMA((3,))],
        )
        field, send = call(
            hop_kernel,
            "hop",
            (routing, table, remote_blocks, far, total),
            (shape((rows, res), BF16), shape((slots, TILE, res), BF16)),
            [SMEM] * 2 + [VMEM] * 2 + [HBM],
            [HBM] * 2,
            hop_flops,
            [thin_field, wide_field, pltpu.SemaphoreType.DMA((3,))],
        )
        far = exchange(send)
        (total,) = call(
            under_second_kernel,
            "under_second",
            (local_table, block_values, field, base, state),
            (shape((rows, res), F32),),
            [SMEM] + [VMEM] * 4,
            [VMEM],
            4 * rows * TILE * res,
        )
    (state,) = call(
        last_kernel,
        "last",
        (table, remote_blocks, far, total),
        (shape((rows, res), BF16),),
        [SMEM] + [VMEM] * 2 + [HBM],
        [HBM],
        hop_flops,
        [thin_field, wide_field, pltpu.SemaphoreType.DMA((2,))],
    )
    return state, skip


def solution(mesh):
    placed = (
        P(("scen", "node"), None),
        P(None, ("scen", "node"), None),
        P(),
        P(),
        P(),
        P(),
        P("node", None, None),
        P("node"),
        P("node"),
        P("node"),
        P("node", None, None),
        P("node", None),
    )
    return jax.shard_map(
        local,
        mesh=mesh,
        in_specs=placed,
        out_specs=(P(("scen", "node"), None), P(("scen", "node"), None)),
        check_vma=False,
    )
```

```python
import functools

import jax
import jax.numpy as jnp
from jax import lax
from jax.experimental import pallas as pl
from jax.experimental.pallas import tpu as pltpu
from jax.sharding import PartitionSpec as P

TILE = 128
CAP = 2
F32 = jnp.float32
BF16 = jnp.bfloat16
VMEM = pl.BlockSpec(memory_space=pltpu.VMEM)
SMEM = pl.BlockSpec(memory_space=pltpu.SMEM)
HBM = pl.BlockSpec(memory_space=pl.ANY)
LIMITS = {"conv_first": 60}
PART = 512


def dot(a, b):
    return jnp.dot(a, b, preferred_element_type=F32)


def call(kernel, name, ins, outs, in_specs, out_specs, flops, scratch=(), alias=None):
    moved = sum(x.size * x.dtype.itemsize for x in ins) + sum(
        o.size * o.dtype.itemsize for o in outs
    )
    return pl.pallas_call(
        kernel,
        name=name,
        out_shape=tuple(outs),
        in_specs=in_specs,
        out_specs=tuple(out_specs),
        scratch_shapes=scratch,
        input_output_aliases=alias or {},
        compiler_params=pltpu.CompilerParams(vmem_limit_bytes=LIMITS.get(name, 52) << 20),
        cost_estimate=pl.CostEstimate(flops=flops, bytes_accessed=moved, transcendentals=0),
    )(*ins)


def shape(dims, dtype):
    return jax.ShapeDtypeStruct(dims, dtype)


def start(source, target, sem):
    copy = pltpu.make_async_copy(source, target, sem)
    copy.start()
    return copy


def start_send(routing, field, send, sem):
    for place in range(send.shape[0]):
        rows = pl.ds(pl.multiple_of(routing[place] * TILE, TILE), TILE)
        start(field.at[rows, :], send.at[place], sem)
    return pltpu.make_async_copy(send, send, sem)


def start_parts(source, target, sem, parts):
    step = source.shape[0] // parts
    for i in range(parts):
        at = pl.ds(i * step, step)
        start(source.at[at, :], target.at[at, :], sem)
    return pltpu.make_async_copy(source, target, sem)


def start_far(table, far, near, sem):
    for j in range(near.shape[0]):
        start(far.at[table[1, j]], near.at[j], sem)
    return pltpu.make_async_copy(near, near, sem)


def add_remote(table, blocks, near, total):
    for j in range(blocks.shape[0]):
        rows = pl.ds(pl.multiple_of(table[0, j] * TILE, TILE), TILE)
        total[rows, :] += dot(blocks[j], near[j])


def convolve(past, state, weight, bias, gated, gated_out, sem, ready=None):
    gate = gated.shape[1]
    for i in range(state.shape[0] // PART):
        at = pl.ds(i * PART, PART)
        if ready is not None:
            ready(i)
        both = jnp.concatenate([past[at, :], state[at, :]], axis=1)
        pre = dot(both, weight[...]) + bias[...]
        value = jnp.tanh(pre[:, :gate]) * (0.5 * jnp.tanh(0.5 * pre[:, gate:]) + 0.5)
        gated[at, :] = value.astype(BF16)
        start(gated.at[at, :], gated_out.at[at, :], sem)
    return pltpu.make_async_copy(gated, gated_out, sem)


def weight_loads(layer, weight_all, bias_all, mix_all, weight, bias, mix, sems):
    depth = mix.shape[0]
    return [
        start(weight_all.at[layer], weight, sems.at[0]),
        start(bias_all.at[pl.ds(layer, 1), :], bias, sems.at[1]),
        start(mix_all.at[layer, pl.ds(2 * depth, depth), :], mix, sems.at[2]),
    ]


def first_kernel(
    routing, state_in, past_all, weight_all, bias_all, mix_all,
    gated_out, send,
    past, weight, bias, mix, gated, second, state, sems, parts, *, layer,
):
    loads = weight_loads(layer, weight_all, bias_all, mix_all, weight, bias, mix, sems)
    pieces = []
    for i in range(state.shape[0] // PART):
        at = pl.ds(i * PART, PART)
        pieces.append(
            (
                start(past_all.at[layer, at, :], past.at[at, :], parts.at[2 * i]),
                start(state_in.at[at, :], state.at[at, :], parts.at[2 * i + 1]),
            )
        )

    def ready(i):
        if i == 0:
            for copy in loads:
                copy.wait()
        for copy in pieces[i]:
            copy.wait()

    copies = [convolve(past, state, weight, bias, gated, gated_out, sems.at[3], ready)]
    second[...] = dot(gated[...], mix[...]).astype(BF16)
    copies.append(start_send(routing, second, send, sems.at[4]))
    for copy in copies:
        copy.wait()


def next_kernel(
    routing, table, blocks, far, total_in, past_all, weight_all, bias_all, mix_all,
    gated_out, send, state_out,
    past, weight, bias, mix, gated, second, state, near, total, sems, *, layer,
):
    inputs = [
        start_far(table, far, near, sems.at[5]),
        start_parts(total_in, total, sems.at[6], 4),
    ]
    loads = weight_loads(layer, weight_all, bias_all, mix_all, weight, bias, mix, sems)
    loads.append(start_parts(past_all.at[layer], past, sems.at[7], 2))
    for copy in inputs:
        copy.wait()
    add_remote(table, blocks, near, total)
    state[...] = total[...].astype(BF16)
    copies = [start_parts(state, state_out, sems.at[8], 2)]
    for copy in loads:
        copy.wait()
    copies.append(convolve(past, state, weight, bias, gated, gated_out, sems.at[3]))
    second[...] = dot(gated[...], mix[...]).astype(BF16)
    copies.append(start_send(routing, second, send, sems.at[4]))
    for copy in copies:
        copy.wait()


def hop_kernel(routing, table, blocks, far, total_in, field_out, send, field, near, total, sems):
    inputs = [
        start_far(table, far, near, sems.at[0]),
        start_parts(total_in, total, sems.at[1], 4),
    ]
    for copy in inputs:
        copy.wait()
    add_remote(table, blocks, near, total)
    field[...] = total[...].astype(BF16)
    copies = [
        start_send(routing, field, send, sems.at[2]),
        start_parts(field, field_out, sems.at[3], 2),
    ]
    for copy in copies:
        copy.wait()


def last_kernel(table, blocks, far, total_in, state_out, state, near, total, sems):
    inputs = [
        start_far(table, far, near, sems.at[0]),
        start_parts(total_in, total, sems.at[1], 4),
    ]
    for copy in inputs:
        copy.wait()
    add_remote(table, blocks, near, total)
    state[...] = total[...].astype(BF16)
    start_parts(state, state_out, sems.at[2], 4).wait()


def build_kernel(place, target, owner, slot, values, table, local, remote_blocks, *, tiles):
    me = place[0]

    def body(b, seen):
        t, o, s = target[b], owner[b], slot[b]
        mine = o == me

        @pl.when(mine)
        def _():
            row = jnp.where(s == t, 0, 1)
            local[row, t] = b
            local[row + 2, t] = s

        @pl.when(jnp.logical_not(mine))
        def _():
            table[0, seen] = t
            table[1, seen] = o * CAP + s
            remote_blocks[seen] = values[b]

        return seen + jnp.where(mine, 0, 1)

    lax.fori_loop(0, target.shape[0], body, jnp.int32(0))


def local_sum(local, values, field, t):
    other = field[pl.ds(pl.multiple_of(local[3, t] * TILE, TILE), TILE), :]
    own = field[pl.ds(t * TILE, TILE), :]
    block = jnp.concatenate([values[local[0, t]], values[local[1, t]]], axis=1)
    return dot(block, jnp.concatenate([own, other], axis=0))


def under_first_kernel(local, values, gated, mix_all, skip_all, *rest, res, layer):
    skip_in = rest[0] if layer else None
    total, base, skip, wide, deep, second, sems = rest[1 if layer else 0 :]
    gate = gated.shape[1]
    loads = [
        start(mix_all.at[layer, pl.ds(2 * gate, gate), :], deep, sems.at[3]),
        start(mix_all.at[layer, pl.ds(gate, gate), :], wide.at[:, pl.ds(0, res)], sems.at[0]),
        start(mix_all.at[layer, pl.ds(0, gate), :], wide.at[:, pl.ds(res, res)], sems.at[1]),
        start(skip_all.at[layer], wide.at[:, pl.ds(2 * res, skip.shape[1])], sems.at[2]),
    ]
    for copy in loads:
        copy.wait()
    second[...] = dot(gated[...], deep[...]).astype(BF16)
    for t in range(gated.shape[0] // TILE):
        at = pl.ds(t * TILE, TILE)
        out = dot(gated[at, :], wide[...])
        total[at, :] = out[:, :res] + local_sum(local, values, second, t)
        base[at, :] = out[:, res : 2 * res]
        gain = out[:, 2 * res :]
        if layer:
            gain = gain + skip_in[at, :]
        skip[at, :] = gain.astype(skip.dtype)


def under_second_kernel(local, values, field, base, state, total):
    for t in range(field.shape[0] // TILE):
        at = pl.ds(t * TILE, TILE)
        total[at, :] = (
            state[at, :].astype(F32) + base[at, :] + local_sum(local, values, field, t)
        )


def local(
    hidden_state,
    conv_cache,
    conv_weight,
    conv_bias,
    mix_weight,
    skip_weight,
    block_values,
    block_target,
    block_owner,
    block_slot,
    send_tiles,
    send_count,
):
    rows, res = hidden_state.shape
    layers = conv_cache.shape[0]
    gate, skips = skip_weight.shape[1:]
    tiles = rows // TILE
    peers = send_tiles.shape[1]
    slots = peers * CAP
    blocks = block_values.shape[0]
    remote = blocks - 2 * tiles
    place = lax.axis_index("node").astype(jnp.int32)[None]
    routing = send_tiles.reshape(slots)

    table, local_table, remote_blocks = call(
        functools.partial(build_kernel, tiles=tiles),
        "sort_blocks",
        (place, block_target, block_owner, block_slot, block_values),
        (
            shape((2, remote), jnp.int32),
            shape((4, tiles), jnp.int32),
            shape((remote, TILE, TILE), BF16),
        ),
        [SMEM] * 4 + [VMEM],
        [SMEM, SMEM, VMEM],
        blocks * 1000,
    )

    def exchange(send):
        got = lax.all_to_all(
            send.reshape(peers, CAP, TILE, res), "node", split_axis=0, concat_axis=0, tiled=True
        )
        return got.reshape(slots, TILE, res)

    conv_flops = 2 * rows * (2 * res * 2 * gate + gate * res)
    hop_flops = 2 * remote * TILE * TILE * res
    conv_outs = (shape((rows, gate), BF16), shape((slots, TILE, res), BF16))
    conv_scratch = [
        pltpu.VMEM((rows, res), BF16),
        pltpu.VMEM((2 * res, 2 * gate), BF16),
        pltpu.VMEM((1, 2 * gate), F32),
        pltpu.VMEM((gate, res), BF16),
        pltpu.VMEM((rows, gate), BF16),
        pltpu.VMEM((rows, res), BF16),
        pltpu.VMEM((rows, res), BF16),
    ]
    near = pltpu.VMEM((remote, TILE, res), BF16)
    wide_field = pltpu.VMEM((rows, res), F32)
    thin_field = pltpu.VMEM((rows, res), BF16)

    def sems(n):
        return pltpu.SemaphoreType.DMA((n,))

    weights = (conv_cache, conv_weight, conv_bias, mix_weight)
    state = hidden_state
    skip = None
    total = far = None
    for layer in range(layers):
        if layer == 0:
            gated, send = call(
                functools.partial(first_kernel, layer=layer),
                "conv_first",
                (routing, state) + weights,
                conv_outs,
                [SMEM] + [HBM] * 5,
                [HBM] * 2,
                conv_flops,
                conv_scratch + [sems(5), sems(2 * rows // PART)],
            )
        else:
            gated, send, state = call(
                functools.partial(next_kernel, layer=layer),
                "conv_next",
                (routing, table, remote_blocks, far, total) + weights,
                conv_outs + (shape((rows, res), BF16),),
                [SMEM] * 2 + [VMEM] + [HBM] * 6,
                [HBM] * 3,
                conv_flops + hop_flops,
                conv_scratch + [near, wide_field, sems(9)],
            )
        far = exchange(send)
        last = layer == layers - 1
        ins = (local_table, block_values, gated, mix_weight, skip_weight)
        if layer:
            ins += (skip,)
        total, base, skip = call(
            functools.partial(under_first_kernel, res=res, layer=layer),
            "under_first",
            ins,
            (
                shape((rows, res), F32),
                shape((rows, res), F32),
                shape((rows, skips), BF16 if last else F32),
            ),
            [SMEM] + [VMEM] * 2 + [HBM] * 2 + [VMEM] * (len(ins) - 5),
            [VMEM] * 3,
            2 * rows * gate * (3 * res + skips) + 4 * rows * TILE * res,
            [
                pltpu.VMEM((gate, 2 * res + skips), BF16),
                pltpu.VMEM((gate, res), BF16),
                thin_field,
                sems(4),
            ],
        )
        field, send = call(
            hop_kernel,
            "hop",
            (routing, table, remote_blocks, far, total),
            (shape((rows, res), BF16), shape((slots, TILE, res), BF16)),
            [SMEM] * 2 + [VMEM] + [HBM] * 2,
            [HBM] * 2,
            hop_flops,
            [thin_field, near, wide_field, sems(4)],
        )
        far = exchange(send)
        (total,) = call(
            under_second_kernel,
            "under_second",
            (local_table, block_values, field, base, state),
            (shape((rows, res), F32),),
            [SMEM] + [VMEM] * 4,
            [VMEM],
            4 * rows * TILE * res,
        )
    (state,) = call(
        last_kernel,
        "last",
        (table, remote_blocks, far, total),
        (shape((rows, res), BF16),),
        [SMEM] + [VMEM] + [HBM] * 2,
        [HBM],
        hop_flops,
        [thin_field, near, wide_field, sems(3)],
    )
    return state, skip


def solution(mesh):
    placed = (
        P(("scen", "node"), None),
        P(None, ("scen", "node"), None),
        P(),
        P(),
        P(),
        P(),
        P("node", None, None),
        P("node"),
        P("node"),
        P("node"),
        P("node", None, None),
        P("node", None),
    )
    return jax.shard_map(
        local,
        mesh=mesh,
        in_specs=placed,
        out_specs=(P(("scen", "node"), None), P(("scen", "node"), None)),
        check_vma=False,
    )
```

```python
import functools

import jax
import jax.numpy as jnp
from jax import lax
from jax.experimental import pallas as pl
from jax.experimental.pallas import tpu as pltpu
from jax.sharding import PartitionSpec as P

TILE = 128
CAP = 2
F32 = jnp.float32
BF16 = jnp.bfloat16
VMEM = pl.BlockSpec(memory_space=pltpu.VMEM)
SMEM = pl.BlockSpec(memory_space=pltpu.SMEM)
HBM = pl.BlockSpec(memory_space=pl.ANY)
LIMITS = {"conv_first": 60}
PART = 512
SECTION = 128
TARGET, SOURCE, PLACE, ROUTE, OWN, OTHER, FROM, SPARE = (SECTION * i for i in range(8))
TABLE = 8 * SECTION
COUNT = TABLE - 1


def dot(a, b):
    return jnp.dot(a, b, preferred_element_type=F32)


def call(kernel, name, ins, outs, in_specs, out_specs, flops, scratch=(), alias=None):
    moved = sum(x.size * x.dtype.itemsize for x in ins) + sum(
        o.size * o.dtype.itemsize for o in outs
    )
    return pl.pallas_call(
        kernel,
        name=name,
        out_shape=tuple(outs),
        in_specs=in_specs,
        out_specs=tuple(out_specs),
        scratch_shapes=scratch,
        input_output_aliases=alias or {},
        compiler_params=pltpu.CompilerParams(vmem_limit_bytes=LIMITS.get(name, 52) << 20),
        cost_estimate=pl.CostEstimate(flops=flops, bytes_accessed=moved, transcendentals=0),
    )(*ins)


def shape(dims, dtype):
    return jax.ShapeDtypeStruct(dims, dtype)


def start(source, target, sem):
    copy = pltpu.make_async_copy(source, target, sem)
    copy.start()
    return copy


def tile_copy(field, tile, send, place, sem):
    rows = pl.ds(pl.multiple_of(tile * TILE, TILE), TILE)
    return pltpu.make_async_copy(field.at[rows, :], send.at[place], sem)


class Sends:
    def __init__(self, table, field, send, sems):
        self.count = table[COUNT]

        def copy(i):
            place = table[PLACE + i]
            return tile_copy(field, table[ROUTE + i], send, place, sems.at[place])

        self.copy = copy
        self.each(lambda i: copy(i).start())

    def each(self, action):
        def body(i, carry):
            action(i)
            return carry

        lax.fori_loop(0, self.count, body, 0)

    def wait(self):
        self.each(lambda i: self.copy(i).wait())


def start_parts(source, target, sem, parts):
    step = source.shape[0] // parts
    for i in range(parts):
        at = pl.ds(i * step, step)
        start(source.at[at, :], target.at[at, :], sem)
    return pltpu.make_async_copy(source, target, sem)


def start_far(table, far, near, sem):
    for j in range(near.shape[0]):
        start(far.at[table[SOURCE + j]], near.at[j], sem)
    return pltpu.make_async_copy(near, near, sem)


def add_remote(table, blocks, near, total):
    for j in range(blocks.shape[0]):
        rows = pl.ds(pl.multiple_of(table[TARGET + j] * TILE, TILE), TILE)
        total[rows, :] += dot(blocks[j], near[j])


def convolve(past, state, weight, bias, gated, gated_out, sem, ready=None):
    gate = gated.shape[1]
    for i in range(state.shape[0] // PART):
        at = pl.ds(i * PART, PART)
        if ready is not None:
            ready(i)
        both = jnp.concatenate([past[at, :], state[at, :]], axis=1)
        pre = dot(both, weight[...]) + bias[...]
        value = jnp.tanh(pre[:, :gate]) * (0.5 * jnp.tanh(0.5 * pre[:, gate:]) + 0.5)
        gated[at, :] = value.astype(BF16)
        start(gated.at[at, :], gated_out.at[at, :], sem)
    return pltpu.make_async_copy(gated, gated_out, sem)


def weight_loads(layer, weight_all, bias_all, mix_all, weight, bias, mix, sems):
    depth = mix.shape[0]
    return [
        start(weight_all.at[layer], weight, sems.at[0]),
        start(bias_all.at[pl.ds(layer, 1), :], bias, sems.at[1]),
        start(mix_all.at[layer, pl.ds(2 * depth, depth), :], mix, sems.at[2]),
    ]


def first_kernel(
    tiles_in, state_in, past_all, weight_all, bias_all, mix_all,
    gated_out, send,
    past, weight, bias, mix, gated, second, state, tiles, sems, parts, *, layer,
):
    loads = weight_loads(layer, weight_all, bias_all, mix_all, weight, bias, mix, sems)
    pieces = []
    for i in range(state.shape[0] // PART):
        at = pl.ds(i * PART, PART)
        pieces.append(
            (
                start(past_all.at[layer, at, :], past.at[at, :], parts.at[2 * i]),
                start(state_in.at[at, :], state.at[at, :], parts.at[2 * i + 1]),
            )
        )
    routes = start(tiles_in, tiles, sems.at[4])

    def ready(i):
        if i == 0:
            for copy in loads:
                copy.wait()
        for copy in pieces[i]:
            copy.wait()

    copies = [convolve(past, state, weight, bias, gated, gated_out, sems.at[3], ready)]
    second[...] = dot(gated[...], mix[...]).astype(BF16)
    routes.wait()
    for place in range(send.shape[0]):
        peer, slot = divmod(place, CAP)
        tile_copy(second, tiles[0, slot, peer], send, place, sems.at[5]).start()
    copies.append(pltpu.make_async_copy(send, send, sems.at[5]))
    for copy in copies:
        copy.wait()


def receive(table_in, far, total_in, table, near, total, sems, more=lambda: None):
    index = start(table_in, table, sems.at[0])
    sums = start_parts(total_in, total, sems.at[1], 4)
    index.wait()
    tiles = start_far(table, far, near, sems.at[2])
    result = more()
    sums.wait()
    tiles.wait()
    return result


def next_kernel(
    table_in, blocks, far, total_in, past_all, weight_all, bias_all, mix_all,
    gated_out, send, state_out,
    past, weight, bias, mix, gated, second, state, table, near, total, arrive, sems, send_sems,
    *, layer,
):
    def more():
        loads = weight_loads(layer, weight_all, bias_all, mix_all, weight, bias, mix, sems)
        loads.append(start_parts(past_all.at[layer], past, sems.at[4], 2))
        return loads

    loads = receive(table_in, far, total_in, table, near, total, arrive, more)
    add_remote(table, blocks, near, total)
    state[...] = total[...].astype(BF16)
    copies = [start_parts(state, state_out, sems.at[5], 2)]
    for copy in loads:
        copy.wait()
    copies.append(convolve(past, state, weight, bias, gated, gated_out, sems.at[3]))
    second[...] = dot(gated[...], mix[...]).astype(BF16)
    copies.append(Sends(table, second, send, send_sems))
    for copy in copies:
        copy.wait()


def hop_kernel(
    table_in, blocks, far, total_in, send, field, table, near, total, arrive, send_sems
):
    receive(table_in, far, total_in, table, near, total, arrive)
    add_remote(table, blocks, near, total)
    field[...] = total[...].astype(BF16)
    Sends(table, field, send, send_sems).wait()


def last_kernel(
    table_in, blocks, far, total_in, state_out, state, table, near, total, arrive, sem
):
    receive(table_in, far, total_in, table, near, total, arrive)
    add_remote(table, blocks, near, total)
    state[...] = total[...].astype(BF16)
    start_parts(state, state_out, sem.at[0], 4).wait()


def build_kernel(place, target, owner, slot, tiles, count, values, table, remote_blocks):
    me = place[0]

    def body(b, seen):
        t, o, s = target[b], owner[b], slot[b]
        mine = o == me

        @pl.when(mine)
        def _():
            table[jnp.where(s == t, OWN, OTHER) + t] = b
            table[jnp.where(s == t, SPARE, FROM) + t] = s

        @pl.when(jnp.logical_not(mine))
        def _():
            table[TARGET + seen] = t
            table[SOURCE + seen] = o * CAP + s
            remote_blocks[seen] = values[b]

        return seen + jnp.where(mine, 0, 1)

    lax.fori_loop(0, target.shape[0], body, jnp.int32(0))
    live = jnp.int32(0)
    for peer in range(tiles.shape[2]):
        for s in range(CAP):
            table[PLACE + live] = peer * CAP + s
            table[ROUTE + live] = tiles[0, s, peer]
            live = live + jnp.where(count[0, peer] > s, 1, 0)
    table[COUNT] = live


def local_sum(table, values, field, t):
    other = field[pl.ds(pl.multiple_of(table[FROM + t] * TILE, TILE), TILE), :]
    own = field[pl.ds(t * TILE, TILE), :]
    block = jnp.concatenate([values[table[OWN + t]], values[table[OTHER + t]]], axis=1)
    return dot(block, jnp.concatenate([own, other], axis=0))


def under_first_kernel(table, values, gated, mix_all, skip_all, *rest, res, layer):
    skip_in = rest[0] if layer else None
    total, base, skip, wide, deep, second, sems = rest[1 if layer else 0 :]
    gate = gated.shape[1]
    loads = [
        start(mix_all.at[layer, pl.ds(2 * gate, gate), :], deep, sems.at[3]),
        start(mix_all.at[layer, pl.ds(gate, gate), :], wide.at[:, pl.ds(0, res)], sems.at[0]),
        start(mix_all.at[layer, pl.ds(0, gate), :], wide.at[:, pl.ds(res, res)], sems.at[1]),
        start(skip_all.at[layer], wide.at[:, pl.ds(2 * res, skip.shape[1])], sems.at[2]),
    ]
    for copy in loads:
        copy.wait()
    second[...] = dot(gated[...], deep[...]).astype(BF16)
    for t in range(gated.shape[0] // TILE):
        at = pl.ds(t * TILE, TILE)
        out = dot(gated[at, :], wide[...])
        total[at, :] = out[:, :res] + local_sum(table, values, second, t)
        base[at, :] = out[:, res : 2 * res]
        gain = out[:, 2 * res :]
        if layer:
            gain = gain + skip_in[at, :]
        skip[at, :] = gain.astype(skip.dtype)


def under_second_kernel(
    table, values, blocks, far, total_in, base, state, total_out, field, near, total, sems
):
    loads = [
        start_far(table, far, near, sems.at[0]),
        start_parts(total_in, total, sems.at[1], 4),
    ]
    for copy in loads:
        copy.wait()
    add_remote(table, blocks, near, total)
    field[...] = total[...].astype(BF16)
    for t in range(field.shape[0] // TILE):
        at = pl.ds(t * TILE, TILE)
        total_out[at, :] = (
            state[at, :].astype(F32) + base[at, :] + local_sum(table, values, field, t)
        )


def local(
    hidden_state,
    conv_cache,
    conv_weight,
    conv_bias,
    mix_weight,
    skip_weight,
    block_values,
    block_target,
    block_owner,
    block_slot,
    send_tiles,
    send_count,
):
    rows, res = hidden_state.shape
    layers = conv_cache.shape[0]
    gate, skips = skip_weight.shape[1:]
    tiles = rows // TILE
    peers = send_tiles.shape[1]
    slots = peers * CAP
    send_tiles = jnp.swapaxes(send_tiles, 1, 2)
    blocks = block_values.shape[0]
    remote = blocks - 2 * tiles
    place = lax.axis_index("node").astype(jnp.int32)[None]
    assert max(slots, remote, tiles) <= SECTION

    table, remote_blocks = call(
        build_kernel,
        "sort_blocks",
        (place, block_target, block_owner, block_slot, send_tiles, send_count, block_values),
        (shape((TABLE,), jnp.int32), shape((remote, TILE, TILE), BF16)),
        [SMEM] * 6 + [VMEM],
        [SMEM, VMEM],
        blocks * 1000,
    )

    def exchange(send):
        got = lax.all_to_all(
            send.reshape(peers, CAP, TILE, res), "node", split_axis=0, concat_axis=0, tiled=True
        )
        return got.reshape(slots, TILE, res)

    conv_flops = 2 * rows * (2 * res * 2 * gate + gate * res)
    hop_flops = 2 * remote * TILE * TILE * res
    conv_outs = (shape((rows, gate), BF16), shape((slots, TILE, res), BF16))
    conv_scratch = [
        pltpu.VMEM((rows, res), BF16),
        pltpu.VMEM((2 * res, 2 * gate), BF16),
        pltpu.VMEM((1, 2 * gate), F32),
        pltpu.VMEM((gate, res), BF16),
        pltpu.VMEM((rows, gate), BF16),
        pltpu.VMEM((rows, res), BF16),
        pltpu.VMEM((rows, res), BF16),
    ]
    near = pltpu.VMEM((remote, TILE, res), BF16)
    wide_field = pltpu.VMEM((rows, res), F32)
    thin_field = pltpu.VMEM((rows, res), BF16)
    index = pltpu.SMEM((TABLE,), jnp.int32)

    def sems(n):
        return pltpu.SemaphoreType.DMA((n,))

    arrival = [index, near, wide_field, sems(3)]
    weights = (conv_cache, conv_weight, conv_bias, mix_weight)
    state = hidden_state
    skip = None
    total = far = None
    for layer in range(layers):
        if layer == 0:
            gated, send = call(
                functools.partial(first_kernel, layer=layer),
                "conv_first",
                (send_tiles, state) + weights,
                conv_outs,
                [HBM] * 6,
                [HBM] * 2,
                conv_flops,
                conv_scratch
                + [
                    pltpu.SMEM(send_tiles.shape, jnp.int32),
                    sems(6),
                    sems(2 * rows // PART),
                ],
            )
        else:
            gated, send, state = call(
                functools.partial(next_kernel, layer=layer),
                "conv_next",
                (table, remote_blocks, far, total) + weights,
                conv_outs + (shape((rows, res), BF16),),
                [HBM, VMEM] + [HBM] * 6,
                [HBM] * 3,
                conv_flops + hop_flops,
                conv_scratch + arrival + [sems(6), sems(slots)],
            )
        far = exchange(send)
        last = layer == layers - 1
        ins = (table, block_values, gated, mix_weight, skip_weight)
        if layer:
            ins += (skip,)
        total, base, skip = call(
            functools.partial(under_first_kernel, res=res, layer=layer),
            "under_first",
            ins,
            (
                shape((rows, res), F32),
                shape((rows, res), F32),
                shape((rows, skips), BF16 if last else F32),
            ),
            [SMEM] + [VMEM] * 2 + [HBM] * 2 + [VMEM] * (len(ins) - 5),
            [VMEM] * 3,
            2 * rows * gate * (3 * res + skips) + 4 * rows * TILE * res,
            [
                pltpu.VMEM((gate, 2 * res + skips), BF16),
                pltpu.VMEM((gate, res), BF16),
                thin_field,
                sems(4),
            ],
        )
        (send,) = call(
            hop_kernel,
            "hop",
            (table, remote_blocks, far, total),
            (shape((slots, TILE, res), BF16),),
            [HBM, VMEM, HBM, HBM],
            [HBM],
            hop_flops,
            [thin_field] + arrival + [sems(slots)],
        )
        near_far, far = far, exchange(send)
        (total,) = call(
            under_second_kernel,
            "under_second",
            (table, block_values, remote_blocks, near_far, total, base, state),
            (shape((rows, res), F32),),
            [SMEM] + [VMEM] * 2 + [HBM] * 2 + [VMEM] * 2,
            [VMEM],
            4 * rows * TILE * res + hop_flops,
            [thin_field, near, wide_field, sems(2)],
        )
    (state,) = call(
        last_kernel,
        "last",
        (table, remote_blocks, far, total),
        (shape((rows, res), BF16),),
        [HBM, VMEM, HBM, HBM],
        [HBM],
        hop_flops,
        [thin_field] + arrival + [sems(1)],
    )
    return state, skip


def solution(mesh):
    placed = (
        P(("scen", "node"), None),
        P(None, ("scen", "node"), None),
        P(),
        P(),
        P(),
        P(),
        P("node", None, None),
        P("node"),
        P("node"),
        P("node"),
        P("node", None, None),
        P("node", None),
    )
    return jax.shard_map(
        local,
        mesh=mesh,
        in_specs=placed,
        out_specs=(P(("scen", "node"), None), P(("scen", "node"), None)),
        check_vma=False,
    )
```

```python
import functools

import jax
import jax.numpy as jnp
from jax import lax
from jax.experimental import pallas as pl
from jax.experimental.pallas import tpu as pltpu
from jax.sharding import PartitionSpec as P

TILE = 128
CAP = 2
F32 = jnp.float32
BF16 = jnp.bfloat16
VMEM = pl.BlockSpec(memory_space=pltpu.VMEM)
SMEM = pl.BlockSpec(memory_space=pltpu.SMEM)
HBM = pl.BlockSpec(memory_space=pl.ANY)
LIMITS = {"conv_first": 60}
PART = 512
SECTION = 128
TARGET, SOURCE, PLACE, ROUTE, OWN, OTHER, FROM, SPARE = (SECTION * i for i in range(8))
TABLE = 8 * SECTION
COUNT = TABLE - 1
GROUP = 4


def dot(a, b):
    return jnp.dot(a, b, preferred_element_type=F32)


def call(kernel, name, ins, outs, in_specs, out_specs, flops, scratch=(), alias=None):
    moved = sum(x.size * x.dtype.itemsize for x in ins) + sum(
        o.size * o.dtype.itemsize for o in outs
    )
    return pl.pallas_call(
        kernel,
        name=name,
        out_shape=tuple(outs),
        in_specs=in_specs,
        out_specs=tuple(out_specs),
        scratch_shapes=scratch,
        input_output_aliases=alias or {},
        compiler_params=pltpu.CompilerParams(vmem_limit_bytes=LIMITS.get(name, 52) << 20),
        cost_estimate=pl.CostEstimate(flops=flops, bytes_accessed=moved, transcendentals=0),
    )(*ins)


def shape(dims, dtype):
    return jax.ShapeDtypeStruct(dims, dtype)


def start(source, target, sem):
    copy = pltpu.make_async_copy(source, target, sem)
    copy.start()
    return copy


def tile_copy(field, tile, send, place, sem):
    rows = pl.ds(pl.multiple_of(tile * TILE, TILE), TILE)
    return pltpu.make_async_copy(field.at[rows, :], send.at[place], sem)


class Sends:
    def __init__(self, table, field, send, sems):
        self.groups = []
        count = table[COUNT]
        for g in range(send.shape[0] // GROUP):
            live = count > g * GROUP

            @pl.when(live)
            def _():
                for i in range(g * GROUP, (g + 1) * GROUP):
                    tile_copy(field, table[ROUTE + i], send, table[PLACE + i], sems.at[g]).start()

            some = send.at[pl.ds(0, GROUP)]
            self.groups.append((live, pltpu.make_async_copy(some, some, sems.at[g])))

    def wait(self):
        for live, copy in self.groups:
            pl.when(live)(copy.wait)


def start_sends(tile_of, field, send, sem):
    for place in range(send.shape[0]):
        tile_copy(field, tile_of(place), send, place, sem).start()
    return pltpu.make_async_copy(send, send, sem)


def start_parts(source, target, sem, parts):
    step = source.shape[0] // parts
    for i in range(parts):
        at = pl.ds(i * step, step)
        start(source.at[at, :], target.at[at, :], sem)
    return pltpu.make_async_copy(source, target, sem)


def start_far(table, far, near, sem):
    for j in range(near.shape[0]):
        start(far.at[table[SOURCE + j]], near.at[j], sem)
    return pltpu.make_async_copy(near, near, sem)


def add_arrived(table, blocks, far, total):
    for j in range(blocks.shape[0]):
        rows = pl.ds(pl.multiple_of(table[TARGET + j] * TILE, TILE), TILE)
        total[rows, :] += dot(blocks[j], far[table[SOURCE + j]])


def add_remote(table, blocks, near, total):
    for j in range(blocks.shape[0]):
        rows = pl.ds(pl.multiple_of(table[TARGET + j] * TILE, TILE), TILE)
        total[rows, :] += dot(blocks[j], near[j])


def convolve(past, state, weight, bias, gated, gated_out, sem, ready=None):
    gate = gated.shape[1]
    for i in range(state.shape[0] // PART):
        at = pl.ds(i * PART, PART)
        if ready is not None:
            ready(i)
        both = jnp.concatenate([past[at, :], state[at, :]], axis=1)
        pre = dot(both, weight[...]) + bias[...]
        value = jnp.tanh(pre[:, :gate]) * (0.5 * jnp.tanh(0.5 * pre[:, gate:]) + 0.5)
        gated[at, :] = value.astype(BF16)
        start(gated.at[at, :], gated_out.at[at, :], sem)
    return pltpu.make_async_copy(gated, gated_out, sem)


def weight_loads(layer, weight_all, bias_all, mix_all, weight, bias, mix, sems):
    depth = mix.shape[0]
    return [
        start(weight_all.at[layer], weight, sems.at[0]),
        start(bias_all.at[pl.ds(layer, 1), :], bias, sems.at[1]),
        start(mix_all.at[layer, pl.ds(2 * depth, depth), :], mix, sems.at[2]),
    ]


def first_kernel(
    tiles_in, state_in, past_all, weight_all, bias_all, mix_all,
    gated_out, send,
    past, weight, bias, mix, gated, second, state, tiles, sems, parts, *, layer,
):
    loads = weight_loads(layer, weight_all, bias_all, mix_all, weight, bias, mix, sems)
    pieces = []
    for i in range(state.shape[0] // PART):
        at = pl.ds(i * PART, PART)
        pieces.append(
            (
                start(past_all.at[layer, at, :], past.at[at, :], parts.at[2 * i]),
                start(state_in.at[at, :], state.at[at, :], parts.at[2 * i + 1]),
            )
        )
    routes = start(tiles_in, tiles, sems.at[4])

    def ready(i):
        if i == 0:
            for copy in loads:
                copy.wait()
        for copy in pieces[i]:
            copy.wait()

    copies = [convolve(past, state, weight, bias, gated, gated_out, sems.at[3], ready)]
    second[...] = dot(gated[...], mix[...]).astype(BF16)
    routes.wait()
    def tile_of(place):
        peer, slot = divmod(place, CAP)
        return tiles[0, slot, peer]

    copies.append(start_sends(tile_of, second, send, sems.at[5]))
    for copy in copies:
        copy.wait()


def receive(table_in, far, part_in, table, part, total, near, sems, more=lambda: None):
    index = start(table_in, table, sems.at[0])
    tiles = start_parts(far, near, sems.at[2], 8)
    sums = start_parts(part_in, part, sems.at[1], 2)
    total[...] = jnp.zeros_like(total)
    result = more()
    index.wait()
    sums.wait()
    tiles.wait()
    return result


def joined(part, total):
    return (part.astype(F32) + total).astype(BF16)


def next_kernel(
    table_in, blocks, far, part_in, past_all, weight_all, bias_all, mix_all,
    gated_out, send,
    past, weight, bias, mix, gated, second, state, table, part, total, near, arrive, sems, send_sems,
    *, layer,
):
    def more():
        loads = weight_loads(layer, weight_all, bias_all, mix_all, weight, bias, mix, sems)
        loads.append(start_parts(past_all.at[layer], past, sems.at[4], 2))
        return loads

    loads = receive(table_in, far, part_in, table, part, total, near, arrive, more)
    add_arrived(table, blocks, near, total)
    state[...] = joined(part[...], total[...])
    for copy in loads:
        copy.wait()
    copies = [convolve(past, state, weight, bias, gated, gated_out, sems.at[3])]
    second[...] = dot(gated[...], mix[...]).astype(BF16)
    copies.append(Sends(table, second, send, send_sems))
    for copy in copies:
        copy.wait()


def hop_kernel(
    table_in, blocks, far, part_in, send, field, table, part, total, near, arrive, send_sems
):
    receive(table_in, far, part_in, table, part, total, near, arrive)
    add_arrived(table, blocks, near, total)
    field[...] = joined(part[...], total[...])
    Sends(table, field, send, send_sems).wait()


def last_kernel(
    table_in, blocks, far, part_in, state_out, state, table, part, total, near, arrive, sem
):
    receive(table_in, far, part_in, table, part, total, near, arrive)
    add_arrived(table, blocks, near, total)
    state[...] = joined(part[...], total[...])
    start_parts(state, state_out, sem.at[0], 4).wait()


def build_kernel(place, target, owner, slot, tiles, count, values, table, remote_blocks):
    me = place[0]

    def body(b, seen):
        t, o, s = target[b], owner[b], slot[b]
        mine = o == me

        @pl.when(mine)
        def _():
            table[jnp.where(s == t, OWN, OTHER) + t] = b
            table[jnp.where(s == t, SPARE, FROM) + t] = s

        @pl.when(jnp.logical_not(mine))
        def _():
            table[TARGET + seen] = t
            table[SOURCE + seen] = o * CAP + s
            remote_blocks[seen] = values[b]

        return seen + jnp.where(mine, 0, 1)

    lax.fori_loop(0, target.shape[0], body, jnp.int32(0))
    slots = tiles.shape[2] * CAP
    live = dead = jnp.int32(0)
    for peer in range(tiles.shape[2]):
        for s in range(CAP):
            used = count[0, peer] > s
            at = jnp.where(used, live, slots - 1 - dead)
            table[PLACE + at] = peer * CAP + s
            table[ROUTE + at] = tiles[0, s, peer]
            live = live + jnp.where(used, 1, 0)
            dead = dead + jnp.where(used, 0, 1)
    table[COUNT] = live


def local_sum(table, values, field, t):
    other = field[pl.ds(pl.multiple_of(table[FROM + t] * TILE, TILE), TILE), :]
    own = field[pl.ds(t * TILE, TILE), :]
    block = jnp.concatenate([values[table[OWN + t]], values[table[OTHER + t]]], axis=1)
    return dot(block, jnp.concatenate([own, other], axis=0))


def under_first_kernel(table, values, gated, mix_all, skip_all, *rest, res, layer):
    if layer:
        skip_in, blocks, far, part_in, *rest = rest
    else:
        state, *rest = rest
    total, base, skip, wide, deep, second, sems = rest[:7]
    gate = gated.shape[1]
    loads = [
        start(mix_all.at[layer, pl.ds(2 * gate, gate), :], deep, sems.at[3]),
        start(mix_all.at[layer, pl.ds(gate, gate), :], wide.at[:, pl.ds(0, res)], sems.at[0]),
        start(mix_all.at[layer, pl.ds(0, gate), :], wide.at[:, pl.ds(res, res)], sems.at[1]),
        start(skip_all.at[layer], wide.at[:, pl.ds(2 * res, skip.shape[1])], sems.at[2]),
    ]
    if layer:
        near, part, sums = rest[7:]
        loads.append(start_far(table, far, near, sems.at[4]))
        loads.append(start_parts(part_in, part, sems.at[5], 4))
        sums[...] = jnp.zeros_like(sums)
    for copy in loads:
        copy.wait()
    if layer:
        add_remote(table, blocks, near, sums)
    second[...] = dot(gated[...], deep[...]).astype(BF16)
    for t in range(gated.shape[0] // TILE):
        at = pl.ds(t * TILE, TILE)
        out = dot(gated[at, :], wide[...])
        total[at, :] = (out[:, :res] + local_sum(table, values, second, t)).astype(BF16)
        now = joined(part[at, :], sums[at, :]) if layer else state[at, :]
        base[at, :] = now.astype(F32) + out[:, res : 2 * res]
        gain = out[:, 2 * res :]
        if layer:
            gain = gain + skip_in[at, :]
        skip[at, :] = gain.astype(skip.dtype)


def under_second_kernel(
    table, values, blocks, far, part_in, base, part_out, field, near, part, total, sems
):
    loads = [
        start_far(table, far, near, sems.at[0]),
        start_parts(part_in, part, sems.at[1], 4),
    ]
    total[...] = jnp.zeros_like(total)
    for copy in loads:
        copy.wait()
    add_remote(table, blocks, near, total)
    field[...] = joined(part[...], total[...])
    for t in range(field.shape[0] // TILE):
        at = pl.ds(t * TILE, TILE)
        part_out[at, :] = (base[at, :] + local_sum(table, values, field, t)).astype(BF16)


def local(
    hidden_state,
    conv_cache,
    conv_weight,
    conv_bias,
    mix_weight,
    skip_weight,
    block_values,
    block_target,
    block_owner,
    block_slot,
    send_tiles,
    send_count,
):
    rows, res = hidden_state.shape
    layers = conv_cache.shape[0]
    gate, skips = skip_weight.shape[1:]
    tiles = rows // TILE
    peers = send_tiles.shape[1]
    slots = peers * CAP
    send_tiles = jnp.swapaxes(send_tiles, 1, 2)
    blocks = block_values.shape[0]
    remote = blocks - 2 * tiles
    place = lax.axis_index("node").astype(jnp.int32)[None]
    assert max(slots, remote, tiles) <= SECTION

    table, remote_blocks = call(
        build_kernel,
        "sort_blocks",
        (place, block_target, block_owner, block_slot, send_tiles, send_count, block_values),
        (shape((TABLE,), jnp.int32), shape((remote, TILE, TILE), BF16)),
        [SMEM] * 6 + [VMEM],
        [SMEM, VMEM],
        blocks * 1000,
    )

    def exchange(send):
        got = lax.all_to_all(
            send.reshape(peers, CAP, TILE, res), "node", split_axis=0, concat_axis=0, tiled=True
        )
        return got.reshape(slots, TILE, res)

    conv_flops = 2 * rows * (2 * res * 2 * gate + gate * res)
    hop_flops = 2 * remote * TILE * TILE * res
    conv_outs = (shape((rows, gate), BF16), shape((slots, TILE, res), BF16))
    conv_scratch = [
        pltpu.VMEM((rows, res), BF16),
        pltpu.VMEM((2 * res, 2 * gate), BF16),
        pltpu.VMEM((1, 2 * gate), F32),
        pltpu.VMEM((gate, res), BF16),
        pltpu.VMEM((rows, gate), BF16),
        pltpu.VMEM((rows, res), BF16),
        pltpu.VMEM((rows, res), BF16),
    ]
    near = pltpu.VMEM((remote, TILE, res), BF16)
    wide_field = pltpu.VMEM((rows, res), F32)
    thin_field = pltpu.VMEM((rows, res), BF16)
    index = pltpu.SMEM((TABLE,), jnp.int32)

    def sems(n):
        return pltpu.SemaphoreType.DMA((n,))

    arrival = [index, thin_field, wide_field, pltpu.VMEM((slots, TILE, res), BF16), sems(3)]
    weights = (conv_cache, conv_weight, conv_bias, mix_weight)
    state = hidden_state
    skip = None
    total = far = None
    for layer in range(layers):
        if layer == 0:
            gated, send = call(
                functools.partial(first_kernel, layer=layer),
                "conv_first",
                (send_tiles, state) + weights,
                conv_outs,
                [HBM] * 6,
                [HBM] * 2,
                conv_flops,
                conv_scratch
                + [
                    pltpu.SMEM(send_tiles.shape, jnp.int32),
                    sems(6),
                    sems(2 * rows // PART),
                ],
            )
        else:
            gated, send = call(
                functools.partial(next_kernel, layer=layer),
                "conv_next",
                (table, remote_blocks, far, total) + weights,
                conv_outs,
                [HBM, VMEM] + [HBM] * 6,
                [HBM] * 2,
                conv_flops + hop_flops,
                conv_scratch + arrival + [sems(6), sems(slots // GROUP)],
            )
        old_far, old_total, far = far, total, exchange(send)
        last = layer == layers - 1
        ins = (table, block_values, gated, mix_weight, skip_weight)
        ins += (skip, remote_blocks, old_far, old_total) if layer else (hidden_state,)
        total, base, skip = call(
            functools.partial(under_first_kernel, res=res, layer=layer),
            "under_first",
            ins,
            (
                shape((rows, res), BF16),
                shape((rows, res), F32),
                shape((rows, skips), BF16 if last else F32),
            ),
            [SMEM] + [VMEM] * 2 + [HBM] * 2 + ([VMEM] * 2 + [HBM] * 2 if layer else [VMEM]),
            [VMEM] * 3,
            2 * rows * gate * (3 * res + skips) + 4 * rows * TILE * res,
            [
                pltpu.VMEM((gate, 2 * res + skips), BF16),
                pltpu.VMEM((gate, res), BF16),
                thin_field,
                sems(6),
            ]
            + ([near, thin_field, wide_field] if layer else []),
        )
        (send,) = call(
            hop_kernel,
            "hop",
            (table, remote_blocks, far, total),
            (shape((slots, TILE, res), BF16),),
            [HBM, VMEM, HBM, HBM],
            [HBM],
            hop_flops,
            [thin_field] + arrival + [sems(slots // GROUP)],
        )
        near_far, far = far, exchange(send)
        (total,) = call(
            under_second_kernel,
            "under_second",
            (table, block_values, remote_blocks, near_far, total, base),
            (shape((rows, res), BF16),),
            [SMEM] + [VMEM] * 2 + [HBM] * 2 + [VMEM],
            [VMEM],
            4 * rows * TILE * res + hop_flops,
            [thin_field, near, thin_field, wide_field, sems(2)],
        )
    (state,) = call(
        last_kernel,
        "last",
        (table, remote_blocks, far, total),
        (shape((rows, res), BF16),),
        [HBM, VMEM, HBM, HBM],
        [HBM],
        hop_flops,
        [thin_field] + arrival + [sems(1)],
    )
    return state, skip


def solution(mesh):
    placed = (
        P(("scen", "node"), None),
        P(None, ("scen", "node"), None),
        P(),
        P(),
        P(),
        P(),
        P("node", None, None),
        P("node"),
        P("node"),
        P("node"),
        P("node", None, None),
        P("node", None),
    )
    return jax.shard_map(
        local,
        mesh=mesh,
        in_specs=placed,
        out_specs=(P(("scen", "node"), None), P(("scen", "node"), None)),
        check_vma=False,
    )
```

```python
import functools

import jax
import jax.numpy as jnp
from jax import lax
from jax.experimental import pallas as pl
from jax.experimental.pallas import tpu as pltpu
from jax.sharding import PartitionSpec as P

TILE = 128
CAP = 2
F32 = jnp.float32
BF16 = jnp.bfloat16
VMEM = pl.BlockSpec(memory_space=pltpu.VMEM)
SMEM = pl.BlockSpec(memory_space=pltpu.SMEM)
HBM = pl.BlockSpec(memory_space=pl.ANY)
LIMITS = {"conv_first": 60, "hop": 50}
PART = 512
SECTION = 128
TARGET, SOURCE, PLACE, ROUTE, OWN, OTHER, FROM, SPARE = (SECTION * i for i in range(8))
TABLE = 8 * SECTION
COUNT = TABLE - 1
GROUP = 4


def dot(a, b):
    return jnp.dot(a, b, preferred_element_type=F32)


def call(kernel, name, ins, outs, in_specs, out_specs, flops, scratch=(), alias=None):
    moved = sum(x.size * x.dtype.itemsize for x in ins) + sum(
        o.size * o.dtype.itemsize for o in outs
    )
    return pl.pallas_call(
        kernel,
        name=name,
        out_shape=tuple(outs),
        in_specs=in_specs,
        out_specs=tuple(out_specs),
        scratch_shapes=scratch,
        input_output_aliases=alias or {},
        compiler_params=pltpu.CompilerParams(vmem_limit_bytes=LIMITS.get(name, 52) << 20),
        cost_estimate=pl.CostEstimate(flops=flops, bytes_accessed=moved, transcendentals=0),
    )(*ins)


def shape(dims, dtype):
    return jax.ShapeDtypeStruct(dims, dtype)


def start(source, target, sem):
    copy = pltpu.make_async_copy(source, target, sem)
    copy.start()
    return copy


def tile_copy(field, tile, send, place, sem):
    rows = pl.ds(pl.multiple_of(tile * TILE, TILE), TILE)
    return pltpu.make_async_copy(field.at[rows, :], send.at[place], sem)


class Sends:
    def __init__(self, table, field, send, sems):
        self.groups = []
        count = table[COUNT]
        for g in range(send.shape[0] // GROUP):
            live = count > g * GROUP

            @pl.when(live)
            def _():
                for i in range(g * GROUP, (g + 1) * GROUP):
                    tile_copy(field, table[ROUTE + i], send, table[PLACE + i], sems.at[g]).start()

            some = send.at[pl.ds(0, GROUP)]
            self.groups.append((live, pltpu.make_async_copy(some, some, sems.at[g])))

    def wait(self):
        for live, copy in self.groups:
            pl.when(live)(copy.wait)


def start_sends(tile_of, field, send, sem):
    for place in range(send.shape[0]):
        tile_copy(field, tile_of(place), send, place, sem).start()
    return pltpu.make_async_copy(send, send, sem)


def start_parts(source, target, sem, parts):
    step = source.shape[0] // parts
    for i in range(parts):
        at = pl.ds(i * step, step)
        start(source.at[at, :], target.at[at, :], sem)
    return pltpu.make_async_copy(source, target, sem)


def start_far(table, far, near, sem):
    for j in range(near.shape[0]):
        start(far.at[table[SOURCE + j]], near.at[j], sem)
    return pltpu.make_async_copy(near, near, sem)


def add_arrived(table, blocks, far, total):
    for j in range(blocks.shape[0]):
        rows = pl.ds(pl.multiple_of(table[TARGET + j] * TILE, TILE), TILE)
        total[rows, :] += dot(blocks[j], far[table[SOURCE + j]])


def add_remote(table, blocks, near, total):
    for j in range(blocks.shape[0]):
        rows = pl.ds(pl.multiple_of(table[TARGET + j] * TILE, TILE), TILE)
        total[rows, :] += dot(blocks[j], near[j])


def convolve(past, state, weight, bias, gated, gated_out, sem, ready=None):
    gate = gated.shape[1]
    for i in range(state.shape[0] // PART):
        at = pl.ds(i * PART, PART)
        if ready is not None:
            ready(i)
        both = jnp.concatenate([past[at, :], state[at, :]], axis=1)
        pre = dot(both, weight[...]) + bias[...]
        value = jnp.tanh(pre[:, :gate]) * (0.5 * jnp.tanh(0.5 * pre[:, gate:]) + 0.5)
        gated[at, :] = value.astype(BF16)
        start(gated.at[at, :], gated_out.at[at, :], sem)
    return pltpu.make_async_copy(gated, gated_out, sem)


def weight_loads(layer, weight_all, bias_all, mix_all, weight, bias, mix, sems):
    depth = mix.shape[0]
    return [
        start(weight_all.at[layer], weight, sems.at[0]),
        start(bias_all.at[pl.ds(layer, 1), :], bias, sems.at[1]),
        start(mix_all.at[layer, pl.ds(2 * depth, depth), :], mix, sems.at[2]),
    ]


def first_kernel(
    tiles_in, state_in, past_all, weight_all, bias_all, mix_all,
    gated_out, send,
    past, weight, bias, mix, gated, second, state, tiles, sems, parts, *, layer,
):
    loads = weight_loads(layer, weight_all, bias_all, mix_all, weight, bias, mix, sems)
    pieces = []
    for i in range(state.shape[0] // PART):
        at = pl.ds(i * PART, PART)
        pieces.append(
            (
                start(past_all.at[layer, at, :], past.at[at, :], parts.at[2 * i]),
                start(state_in.at[at, :], state.at[at, :], parts.at[2 * i + 1]),
            )
        )
    routes = start(tiles_in, tiles, sems.at[4])

    def ready(i):
        if i == 0:
            for copy in loads:
                copy.wait()
        for copy in pieces[i]:
            copy.wait()

    copies = [convolve(past, state, weight, bias, gated, gated_out, sems.at[3], ready)]
    second[...] = dot(gated[...], mix[...]).astype(BF16)
    routes.wait()
    def tile_of(place):
        peer, slot = divmod(place, CAP)
        return tiles[0, slot, peer]

    copies.append(start_sends(tile_of, second, send, sems.at[5]))
    for copy in copies:
        copy.wait()


def receive(table_in, part_in, table, part, total, sems, more=lambda: None, far=None, near=None):
    waits = [start(table_in, table, sems.at[0])]
    if near is not None:
        waits.append(start_parts(far, near, sems.at[2], 8))
    waits.append(start_parts(part_in, part, sems.at[1], 2))
    total[...] = jnp.zeros_like(total)
    result = more()
    for copy in waits:
        copy.wait()
    return result


def joined(part, total):
    return (part.astype(F32) + total).astype(BF16)


def next_kernel(
    table_in, blocks, far, part_in, past_all, weight_all, bias_all, mix_all,
    gated_out, send,
    past, weight, bias, mix, gated, second, state, table, part, total, near, arrive, sems, send_sems,
    *, layer,
):
    def more():
        loads = weight_loads(layer, weight_all, bias_all, mix_all, weight, bias, mix, sems)
        loads.append(start_parts(past_all.at[layer], past, sems.at[4], 2))
        return loads

    loads = receive(table_in, part_in, table, part, total, arrive, more, far, near)
    add_arrived(table, blocks, near, total)
    state[...] = joined(part[...], total[...])
    for copy in loads:
        copy.wait()
    copies = [convolve(past, state, weight, bias, gated, gated_out, sems.at[3])]
    second[...] = dot(gated[...], mix[...]).astype(BF16)
    copies.append(Sends(table, second, send, send_sems))
    for copy in copies:
        copy.wait()


def hop_kernel(
    table_in, blocks, far, part_in, send, field, table, part, total, arrive, send_sems
):
    receive(table_in, part_in, table, part, total, arrive)
    add_arrived(table, blocks, far, total)
    field[...] = joined(part[...], total[...])
    Sends(table, field, send, send_sems).wait()


def last_kernel(
    table_in, blocks, far, part_in, state_out, state, table, part, total, near, arrive, sem
):
    receive(table_in, part_in, table, part, total, arrive, far=far, near=near)
    add_arrived(table, blocks, near, total)
    state[...] = joined(part[...], total[...])
    start_parts(state, state_out, sem.at[0], 4).wait()


def build_kernel(place, target, owner, slot, tiles, count, values, table, remote_blocks):
    me = place[0]

    def body(b, seen):
        t, o, s = target[b], owner[b], slot[b]
        mine = o == me

        @pl.when(mine)
        def _():
            table[jnp.where(s == t, OWN, OTHER) + t] = b
            table[jnp.where(s == t, SPARE, FROM) + t] = s

        @pl.when(jnp.logical_not(mine))
        def _():
            table[TARGET + seen] = t
            table[SOURCE + seen] = o * CAP + s
            remote_blocks[seen] = values[b]

        return seen + jnp.where(mine, 0, 1)

    lax.fori_loop(0, target.shape[0], body, jnp.int32(0))
    slots = tiles.shape[2] * CAP
    live = dead = jnp.int32(0)
    for peer in range(tiles.shape[2]):
        for s in range(CAP):
            used = count[0, peer] > s
            at = jnp.where(used, live, slots - 1 - dead)
            table[PLACE + at] = peer * CAP + s
            table[ROUTE + at] = tiles[0, s, peer]
            live = live + jnp.where(used, 1, 0)
            dead = dead + jnp.where(used, 0, 1)
    table[COUNT] = live


def local_sum(table, values, field, t):
    other = field[pl.ds(pl.multiple_of(table[FROM + t] * TILE, TILE), TILE), :]
    own = field[pl.ds(t * TILE, TILE), :]
    block = jnp.concatenate([values[table[OWN + t]], values[table[OTHER + t]]], axis=1)
    return dot(block, jnp.concatenate([own, other], axis=0))


def under_first_kernel(table, values, gated, mix_all, skip_all, *rest, res, layer):
    if layer:
        skip_in, blocks, far, part_in, *rest = rest
    else:
        state, *rest = rest
    total, base, skip, wide, deep, second, sems = rest[:7]
    gate = gated.shape[1]
    loads = [
        start(mix_all.at[layer, pl.ds(2 * gate, gate), :], deep, sems.at[3]),
        start(mix_all.at[layer, pl.ds(gate, gate), :], wide.at[:, pl.ds(0, res)], sems.at[0]),
        start(mix_all.at[layer, pl.ds(0, gate), :], wide.at[:, pl.ds(res, res)], sems.at[1]),
        start(skip_all.at[layer], wide.at[:, pl.ds(2 * res, skip.shape[1])], sems.at[2]),
    ]
    if layer:
        near, part, sums = rest[7:]
        loads.append(start_far(table, far, near, sems.at[4]))
        loads.append(start_parts(part_in, part, sems.at[5], 4))
        sums[...] = jnp.zeros_like(sums)
    for copy in loads:
        copy.wait()
    if layer:
        add_remote(table, blocks, near, sums)
    second[...] = dot(gated[...], deep[...]).astype(BF16)
    for t in range(gated.shape[0] // TILE):
        at = pl.ds(t * TILE, TILE)
        out = dot(gated[at, :], wide[...])
        total[at, :] = (out[:, :res] + local_sum(table, values, second, t)).astype(BF16)
        now = joined(part[at, :], sums[at, :]) if layer else state[at, :]
        base[at, :] = now.astype(F32) + out[:, res : 2 * res]
        gain = out[:, 2 * res :]
        if layer:
            gain = gain + skip_in[at, :]
        skip[at, :] = gain.astype(skip.dtype)


def under_second_kernel(
    table, values, blocks, far, part_in, base, part_out, field, near, part, total, sems
):
    loads = [
        start_far(table, far, near, sems.at[0]),
        start_parts(part_in, part, sems.at[1], 4),
    ]
    total[...] = jnp.zeros_like(total)
    for copy in loads:
        copy.wait()
    add_remote(table, blocks, near, total)
    field[...] = joined(part[...], total[...])
    for t in range(field.shape[0] // TILE):
        at = pl.ds(t * TILE, TILE)
        part_out[at, :] = (base[at, :] + local_sum(table, values, field, t)).astype(BF16)


def local(
    hidden_state,
    conv_cache,
    conv_weight,
    conv_bias,
    mix_weight,
    skip_weight,
    block_values,
    block_target,
    block_owner,
    block_slot,
    send_tiles,
    send_count,
):
    rows, res = hidden_state.shape
    layers = conv_cache.shape[0]
    gate, skips = skip_weight.shape[1:]
    tiles = rows // TILE
    peers = send_tiles.shape[1]
    slots = peers * CAP
    send_tiles = jnp.swapaxes(send_tiles, 1, 2)
    blocks = block_values.shape[0]
    remote = blocks - 2 * tiles
    place = lax.axis_index("node").astype(jnp.int32)[None]
    assert max(slots, remote, tiles) <= SECTION

    table, remote_blocks = call(
        build_kernel,
        "sort_blocks",
        (place, block_target, block_owner, block_slot, send_tiles, send_count, block_values),
        (shape((TABLE,), jnp.int32), shape((remote, TILE, TILE), BF16)),
        [SMEM] * 6 + [VMEM],
        [SMEM, VMEM],
        blocks * 1000,
    )

    def exchange(send):
        got = lax.all_to_all(
            send.reshape(peers, CAP, TILE, res), "node", split_axis=0, concat_axis=0, tiled=True
        )
        return got.reshape(slots, TILE, res)

    conv_flops = 2 * rows * (2 * res * 2 * gate + gate * res)
    hop_flops = 2 * remote * TILE * TILE * res
    conv_outs = (shape((rows, gate), BF16), shape((slots, TILE, res), BF16))
    conv_scratch = [
        pltpu.VMEM((rows, res), BF16),
        pltpu.VMEM((2 * res, 2 * gate), BF16),
        pltpu.VMEM((1, 2 * gate), F32),
        pltpu.VMEM((gate, res), BF16),
        pltpu.VMEM((rows, gate), BF16),
        pltpu.VMEM((rows, res), BF16),
        pltpu.VMEM((rows, res), BF16),
    ]
    near = pltpu.VMEM((remote, TILE, res), BF16)
    wide_field = pltpu.VMEM((rows, res), F32)
    thin_field = pltpu.VMEM((rows, res), BF16)
    index = pltpu.SMEM((TABLE,), jnp.int32)

    def sems(n):
        return pltpu.SemaphoreType.DMA((n,))

    arrival = [index, thin_field, wide_field, pltpu.VMEM((slots, TILE, res), BF16), sems(3)]
    direct_arrival = [index, thin_field, wide_field, sems(2)]
    weights = (conv_cache, conv_weight, conv_bias, mix_weight)
    state = hidden_state
    skip = None
    total = far = None
    for layer in range(layers):
        if layer == 0:
            gated, send = call(
                functools.partial(first_kernel, layer=layer),
                "conv_first",
                (send_tiles, state) + weights,
                conv_outs,
                [HBM] * 6,
                [HBM] * 2,
                conv_flops,
                conv_scratch
                + [
                    pltpu.SMEM(send_tiles.shape, jnp.int32),
                    sems(6),
                    sems(2 * rows // PART),
                ],
            )
        else:
            gated, send = call(
                functools.partial(next_kernel, layer=layer),
                "conv_next",
                (table, remote_blocks, far, total) + weights,
                conv_outs,
                [HBM, VMEM] + [HBM] * 6,
                [HBM] * 2,
                conv_flops + hop_flops,
                conv_scratch + arrival + [sems(6), sems(slots // GROUP)],
            )
        old_far, old_total, far = far, total, exchange(send)
        last = layer == layers - 1
        ins = (table, block_values, gated, mix_weight, skip_weight)
        ins += (skip, remote_blocks, old_far, old_total) if layer else (hidden_state,)
        total, base, skip = call(
            functools.partial(under_first_kernel, res=res, layer=layer),
            "under_first",
            ins,
            (
                shape((rows, res), BF16),
                shape((rows, res), F32),
                shape((rows, skips), BF16 if last else F32),
            ),
            [SMEM] + [VMEM] * 2 + [HBM] * 2 + ([VMEM] * 2 + [HBM] * 2 if layer else [VMEM]),
            [VMEM] * 3,
            2 * rows * gate * (3 * res + skips) + 4 * rows * TILE * res,
            [
                pltpu.VMEM((gate, 2 * res + skips), BF16),
                pltpu.VMEM((gate, res), BF16),
                thin_field,
                sems(6),
            ]
            + ([near, thin_field, wide_field] if layer else []),
        )
        (send,) = call(
            hop_kernel,
            "hop",
            (table, remote_blocks, far, total),
            (shape((slots, TILE, res), BF16),),
            [HBM, VMEM, VMEM, HBM],
            [HBM],
            hop_flops,
            [thin_field] + direct_arrival + [sems(slots // GROUP)],
        )
        near_far, far = far, exchange(send)
        (total,) = call(
            under_second_kernel,
            "under_second",
            (table, block_values, remote_blocks, near_far, total, base),
            (shape((rows, res), BF16),),
            [SMEM] + [VMEM] * 2 + [HBM] * 2 + [VMEM],
            [VMEM],
            4 * rows * TILE * res + hop_flops,
            [thin_field, near, thin_field, wide_field, sems(2)],
        )
    (state,) = call(
        last_kernel,
        "last",
        (table, remote_blocks, far, total),
        (shape((rows, res), BF16),),
        [HBM, VMEM, HBM, HBM],
        [HBM],
        hop_flops,
        [thin_field] + arrival + [sems(1)],
    )
    return state, skip


def solution(mesh):
    placed = (
        P(("scen", "node"), None),
        P(None, ("scen", "node"), None),
        P(),
        P(),
        P(),
        P(),
        P("node", None, None),
        P("node"),
        P("node"),
        P("node"),
        P("node", None, None),
        P("node", None),
    )
    return jax.shard_map(
        local,
        mesh=mesh,
        in_specs=placed,
        out_specs=(P(("scen", "node"), None), P(("scen", "node"), None)),
        check_vma=False,
    )
```

```python
import functools

import jax
import jax.numpy as jnp
from jax import lax
from jax.experimental import pallas as pl
from jax.experimental.pallas import tpu as pltpu
from jax.sharding import PartitionSpec as P

TILE = 128
CAP = 2
F32 = jnp.float32
BF16 = jnp.bfloat16
VMEM = pl.BlockSpec(memory_space=pltpu.VMEM)
SMEM = pl.BlockSpec(memory_space=pltpu.SMEM)
HBM = pl.BlockSpec(memory_space=pl.ANY)
LIMITS = {"conv_first": 60, "hop": 50}
PART = 512
SECTION = 128
TARGET, SOURCE, PLACE, ROUTE, OWN, OTHER, FROM, SPARE = (SECTION * i for i in range(8))
TABLE = 8 * SECTION
COUNT = TABLE - 1
GROUP = 4


def dot(a, b):
    return jnp.dot(a, b, preferred_element_type=F32)


def call(kernel, name, ins, outs, in_specs, out_specs, flops, scratch=(), alias=None):
    moved = sum(x.size * x.dtype.itemsize for x in ins) + sum(
        o.size * o.dtype.itemsize for o in outs
    )
    return pl.pallas_call(
        kernel,
        name=name,
        out_shape=tuple(outs),
        in_specs=in_specs,
        out_specs=tuple(out_specs),
        scratch_shapes=scratch,
        input_output_aliases=alias or {},
        compiler_params=pltpu.CompilerParams(vmem_limit_bytes=LIMITS.get(name, 52) << 20),
        cost_estimate=pl.CostEstimate(flops=flops, bytes_accessed=moved, transcendentals=0),
    )(*ins)


def shape(dims, dtype):
    return jax.ShapeDtypeStruct(dims, dtype)


def start(source, target, sem):
    copy = pltpu.make_async_copy(source, target, sem)
    copy.start()
    return copy


def tile_copy(field, tile, send, place, sem):
    rows = pl.ds(pl.multiple_of(tile * TILE, TILE), TILE)
    return pltpu.make_async_copy(field.at[rows, :], send.at[place], sem)


class Sends:
    def __init__(self, table, field, send, sems):
        self.groups = []
        count = table[COUNT]
        for g in range(send.shape[0] // GROUP):
            live = count > g * GROUP

            @pl.when(live)
            def _():
                for i in range(g * GROUP, (g + 1) * GROUP):
                    tile_copy(field, table[ROUTE + i], send, table[PLACE + i], sems.at[g]).start()

            some = send.at[pl.ds(0, GROUP)]
            self.groups.append((live, pltpu.make_async_copy(some, some, sems.at[g])))

    def wait(self):
        for live, copy in self.groups:
            pl.when(live)(copy.wait)


def start_sends(tile_of, field, send, sem):
    for place in range(send.shape[0]):
        tile_copy(field, tile_of(place), send, place, sem).start()
    return pltpu.make_async_copy(send, send, sem)


def start_parts(source, target, sem, parts):
    step = source.shape[0] // parts
    for i in range(parts):
        at = pl.ds(i * step, step)
        start(source.at[at, :], target.at[at, :], sem)
    return pltpu.make_async_copy(source, target, sem)


def start_far(table, far, near, sem):
    for j in range(near.shape[0]):
        start(far.at[table[SOURCE + j]], near.at[j], sem)
    return pltpu.make_async_copy(near, near, sem)


def add_arrived(table, blocks, far, total):
    for j in range(blocks.shape[0]):
        rows = pl.ds(pl.multiple_of(table[TARGET + j] * TILE, TILE), TILE)
        total[rows, :] += dot(blocks[j], far[table[SOURCE + j]])


def add_remote(table, blocks, near, total):
    for j in range(blocks.shape[0]):
        rows = pl.ds(pl.multiple_of(table[TARGET + j] * TILE, TILE), TILE)
        total[rows, :] += dot(blocks[j], near[j])


def convolve(past, state, weight, bias, gated, gated_out, sem, ready=None):
    gate = gated.shape[1]
    for i in range(state.shape[0] // PART):
        at = pl.ds(i * PART, PART)
        if ready is not None:
            ready(i)
        both = jnp.concatenate([past[at, :], state[at, :]], axis=1)
        pre = dot(both, weight[...]) + bias[...]
        value = jnp.tanh(pre[:, :gate]) * (0.5 * jnp.tanh(0.5 * pre[:, gate:]) + 0.5)
        gated[at, :] = value.astype(BF16)
        start(gated.at[at, :], gated_out.at[at, :], sem)
    return pltpu.make_async_copy(gated, gated_out, sem)


def weight_loads(layer, weight_all, bias_all, mix_all, weight, bias, mix, sems):
    depth = mix.shape[0]
    return [
        start(weight_all.at[layer], weight, sems.at[0]),
        start(bias_all.at[pl.ds(layer, 1), :], bias, sems.at[1]),
        start(mix_all.at[layer, pl.ds(2 * depth, depth), :], mix, sems.at[2]),
    ]


def first_kernel(
    tiles_in, state_in, past_all, weight_all, bias_all, mix_all,
    gated_out, send,
    past, weight, bias, mix, gated, second, state, tiles, sems, parts, *, layer,
):
    loads = weight_loads(layer, weight_all, bias_all, mix_all, weight, bias, mix, sems)
    pieces = []
    for i in range(state.shape[0] // PART):
        at = pl.ds(i * PART, PART)
        pieces.append(
            (
                start(past_all.at[layer, at, :], past.at[at, :], parts.at[2 * i]),
                start(state_in.at[at, :], state.at[at, :], parts.at[2 * i + 1]),
            )
        )
    routes = start(tiles_in, tiles, sems.at[4])

    def ready(i):
        if i == 0:
            for copy in loads:
                copy.wait()
        for copy in pieces[i]:
            copy.wait()

    copies = [convolve(past, state, weight, bias, gated, gated_out, sems.at[3], ready)]
    second[...] = dot(gated[...], mix[...]).astype(BF16)
    routes.wait()
    def tile_of(place):
        peer, slot = divmod(place, CAP)
        return tiles[0, slot, peer]

    copies.append(start_sends(tile_of, second, send, sems.at[5]))
    for copy in copies:
        copy.wait()


def receive(table_in, part_in, table, part, total, sems, more=lambda: None, far=None, near=None):
    waits = [start(table_in, table, sems.at[0])]
    if near is not None:
        waits.append(start_parts(far, near, sems.at[2], 4))
    waits.append(start_parts(part_in, part, sems.at[1], 1))
    total[...] = jnp.zeros_like(total)
    result = more()
    for copy in waits:
        copy.wait()
    return result


def joined(part, total):
    return (part.astype(F32) + total).astype(BF16)


def next_kernel(
    table_in, blocks, far, part_in, past_all, weight_all, bias_all, mix_all,
    gated_out, send,
    past, weight, bias, mix, gated, second, state, table, part, total, near, arrive, sems, send_sems,
    *, layer,
):
    def more():
        loads = weight_loads(layer, weight_all, bias_all, mix_all, weight, bias, mix, sems)
        loads.append(start_parts(past_all.at[layer], past, sems.at[4], 1))
        return loads

    loads = receive(table_in, part_in, table, part, total, arrive, more, far, near)
    add_arrived(table, blocks, near, total)
    state[...] = joined(part[...], total[...])
    for copy in loads:
        copy.wait()
    copies = [convolve(past, state, weight, bias, gated, gated_out, sems.at[3])]
    second[...] = dot(gated[...], mix[...]).astype(BF16)
    copies.append(Sends(table, second, send, send_sems))
    for copy in copies:
        copy.wait()


def hop_kernel(
    table_in, blocks, far, part_in, send, field, table, part, total, arrive, send_sems
):
    receive(table_in, part_in, table, part, total, arrive)
    add_arrived(table, blocks, far, total)
    field[...] = joined(part[...], total[...])
    Sends(table, field, send, send_sems).wait()


def last_kernel(
    table_in, blocks, far, part_in, state_out, state, table, part, total, near, arrive, sem
):
    receive(table_in, part_in, table, part, total, arrive, far=far, near=near)
    add_arrived(table, blocks, near, total)
    state[...] = joined(part[...], total[...])
    start_parts(state, state_out, sem.at[0], 2).wait()


def build_kernel(place, target, owner, slot, tiles, count, values, table, remote_blocks):
    me = place[0]

    def body(b, seen):
        t, o, s = target[b], owner[b], slot[b]
        mine = o == me

        @pl.when(mine)
        def _():
            table[jnp.where(s == t, OWN, OTHER) + t] = b
            table[jnp.where(s == t, SPARE, FROM) + t] = s

        @pl.when(jnp.logical_not(mine))
        def _():
            table[TARGET + seen] = t
            table[SOURCE + seen] = o * CAP + s
            remote_blocks[seen] = values[b]

        return seen + jnp.where(mine, 0, 1)

    lax.fori_loop(0, target.shape[0], body, jnp.int32(0))
    slots = tiles.shape[2] * CAP
    live = dead = jnp.int32(0)
    for peer in range(tiles.shape[2]):
        for s in range(CAP):
            used = count[0, peer] > s
            at = jnp.where(used, live, slots - 1 - dead)
            table[PLACE + at] = peer * CAP + s
            table[ROUTE + at] = tiles[0, s, peer]
            live = live + jnp.where(used, 1, 0)
            dead = dead + jnp.where(used, 0, 1)
    table[COUNT] = live


def local_sum(table, values, field, t):
    other = field[pl.ds(pl.multiple_of(table[FROM + t] * TILE, TILE), TILE), :]
    own = field[pl.ds(t * TILE, TILE), :]
    block = jnp.concatenate([values[table[OWN + t]], values[table[OTHER + t]]], axis=1)
    return dot(block, jnp.concatenate([own, other], axis=0))


def under_first_kernel(table, values, gated, mix_all, skip_all, *rest, res, layer):
    if layer:
        skip_in, blocks, far, part_in, *rest = rest
    else:
        state, *rest = rest
    total, base, skip, wide, deep, second, sems = rest[:7]
    gate = gated.shape[1]
    loads = [
        start(mix_all.at[layer, pl.ds(2 * gate, gate), :], deep, sems.at[3]),
        start(mix_all.at[layer, pl.ds(gate, gate), :], wide.at[:, pl.ds(0, res)], sems.at[0]),
        start(mix_all.at[layer, pl.ds(0, gate), :], wide.at[:, pl.ds(res, res)], sems.at[1]),
        start(skip_all.at[layer], wide.at[:, pl.ds(2 * res, skip.shape[1])], sems.at[2]),
    ]
    if layer:
        near, part, sums = rest[7:]
        loads.append(start_far(table, far, near, sems.at[4]))
        loads.append(start_parts(part_in, part, sems.at[5], 4))
        sums[...] = jnp.zeros_like(sums)
    for copy in loads:
        copy.wait()
    if layer:
        add_remote(table, blocks, near, sums)
    second[...] = dot(gated[...], deep[...]).astype(BF16)
    for t in range(gated.shape[0] // TILE):
        at = pl.ds(t * TILE, TILE)
        out = dot(gated[at, :], wide[...])
        total[at, :] = (out[:, :res] + local_sum(table, values, second, t)).astype(BF16)
        now = joined(part[at, :], sums[at, :]) if layer else state[at, :]
        base[at, :] = now.astype(F32) + out[:, res : 2 * res]
        gain = out[:, 2 * res :]
        if layer:
            gain = gain + skip_in[at, :]
        skip[at, :] = gain.astype(skip.dtype)


def under_second_kernel(
    table, values, blocks, far, part_in, base, part_out, field, near, part, total, sems
):
    loads = [
        start_far(table, far, near, sems.at[0]),
        start_parts(part_in, part, sems.at[1], 4),
    ]
    total[...] = jnp.zeros_like(total)
    for copy in loads:
        copy.wait()
    add_remote(table, blocks, near, total)
    field[...] = joined(part[...], total[...])
    for t in range(field.shape[0] // TILE):
        at = pl.ds(t * TILE, TILE)
        part_out[at, :] = (base[at, :] + local_sum(table, values, field, t)).astype(BF16)


def local(
    hidden_state,
    conv_cache,
    conv_weight,
    conv_bias,
    mix_weight,
    skip_weight,
    block_values,
    block_target,
    block_owner,
    block_slot,
    send_tiles,
    send_count,
):
    rows, res = hidden_state.shape
    layers = conv_cache.shape[0]
    gate, skips = skip_weight.shape[1:]
    tiles = rows // TILE
    peers = send_tiles.shape[1]
    slots = peers * CAP
    send_tiles = jnp.swapaxes(send_tiles, 1, 2)
    blocks = block_values.shape[0]
    remote = blocks - 2 * tiles
    place = lax.axis_index("node").astype(jnp.int32)[None]
    assert max(slots, remote, tiles) <= SECTION

    table, remote_blocks = call(
        build_kernel,
        "sort_blocks",
        (place, block_target, block_owner, block_slot, send_tiles, send_count, block_values),
        (shape((TABLE,), jnp.int32), shape((remote, TILE, TILE), BF16)),
        [SMEM] * 6 + [VMEM],
        [SMEM, VMEM],
        blocks * 1000,
    )

    def exchange(send):
        got = lax.all_to_all(
            send.reshape(peers, CAP, TILE, res), "node", split_axis=0, concat_axis=0, tiled=True
        )
        return got.reshape(slots, TILE, res)

    conv_flops = 2 * rows * (2 * res * 2 * gate + gate * res)
    hop_flops = 2 * remote * TILE * TILE * res
    conv_outs = (shape((rows, gate), BF16), shape((slots, TILE, res), BF16))
    conv_scratch = [
        pltpu.VMEM((rows, res), BF16),
        pltpu.VMEM((2 * res, 2 * gate), BF16),
        pltpu.VMEM((1, 2 * gate), F32),
        pltpu.VMEM((gate, res), BF16),
        pltpu.VMEM((rows, gate), BF16),
        pltpu.VMEM((rows, res), BF16),
        pltpu.VMEM((rows, res), BF16),
    ]
    near = pltpu.VMEM((remote, TILE, res), BF16)
    wide_field = pltpu.VMEM((rows, res), F32)
    thin_field = pltpu.VMEM((rows, res), BF16)
    index = pltpu.SMEM((TABLE,), jnp.int32)

    def sems(n):
        return pltpu.SemaphoreType.DMA((n,))

    arrival = [index, thin_field, wide_field, pltpu.VMEM((slots, TILE, res), BF16), sems(3)]
    direct_arrival = [index, thin_field, wide_field, sems(2)]
    weights = (conv_cache, conv_weight, conv_bias, mix_weight)
    state = hidden_state
    skip = None
    total = far = None
    for layer in range(layers):
        if layer == 0:
            gated, send = call(
                functools.partial(first_kernel, layer=layer),
                "conv_first",
                (send_tiles, state) + weights,
                conv_outs,
                [HBM] * 6,
                [HBM] * 2,
                conv_flops,
                conv_scratch
                + [
                    pltpu.SMEM(send_tiles.shape, jnp.int32),
                    sems(6),
                    sems(2 * rows // PART),
                ],
            )
        else:
            gated, send = call(
                functools.partial(next_kernel, layer=layer),
                "conv_next",
                (table, remote_blocks, far, total) + weights,
                conv_outs,
                [HBM, VMEM] + [HBM] * 6,
                [HBM] * 2,
                conv_flops + hop_flops,
                conv_scratch + arrival + [sems(6), sems(slots // GROUP)],
            )
        old_far, old_total, far = far, total, exchange(send)
        last = layer == layers - 1
        ins = (table, block_values, gated, mix_weight, skip_weight)
        ins += (skip, remote_blocks, old_far, old_total) if layer else (hidden_state,)
        total, base, skip = call(
            functools.partial(under_first_kernel, res=res, layer=layer),
            "under_first",
            ins,
            (
                shape((rows, res), BF16),
                shape((rows, res), F32),
                shape((rows, skips), BF16 if last else F32),
            ),
            [SMEM] + [VMEM] * 2 + [HBM] * 2 + ([VMEM] * 2 + [HBM] * 2 if layer else [VMEM]),
            [VMEM] * 3,
            2 * rows * gate * (3 * res + skips) + 4 * rows * TILE * res,
            [
                pltpu.VMEM((gate, 2 * res + skips), BF16),
                pltpu.VMEM((gate, res), BF16),
                thin_field,
                sems(6),
            ]
            + ([near, thin_field, wide_field] if layer else []),
        )
        (send,) = call(
            hop_kernel,
            "hop",
            (table, remote_blocks, far, total),
            (shape((slots, TILE, res), BF16),),
            [HBM, VMEM, VMEM, HBM],
            [HBM],
            hop_flops,
            [thin_field] + direct_arrival + [sems(slots // GROUP)],
        )
        near_far, far = far, exchange(send)
        (total,) = call(
            under_second_kernel,
            "under_second",
            (table, block_values, remote_blocks, near_far, total, base),
            (shape((rows, res), BF16),),
            [SMEM] + [VMEM] * 2 + [HBM] * 2 + [VMEM],
            [VMEM],
            4 * rows * TILE * res + hop_flops,
            [thin_field, near, thin_field, wide_field, sems(2)],
        )
    (state,) = call(
        last_kernel,
        "last",
        (table, remote_blocks, far, total),
        (shape((rows, res), BF16),),
        [HBM, VMEM, HBM, HBM],
        [HBM],
        hop_flops,
        [thin_field] + arrival + [sems(1)],
    )
    return state, skip


def solution(mesh):
    placed = (
        P(("scen", "node"), None),
        P(None, ("scen", "node"), None),
        P(),
        P(),
        P(),
        P(),
        P("node", None, None),
        P("node"),
        P("node"),
        P("node"),
        P("node", None, None),
        P("node", None),
    )
    return jax.shard_map(
        local,
        mesh=mesh,
        in_specs=placed,
        out_specs=(P(("scen", "node"), None), P(("scen", "node"), None)),
        check_vma=False,
    )
```

```python
import functools

import jax
import jax.numpy as jnp
from jax import lax
from jax.experimental import pallas as pl
from jax.experimental.pallas import tpu as pltpu
from jax.sharding import PartitionSpec as P

TILE = 128
CAP = 2
F32 = jnp.float32
BF16 = jnp.bfloat16
VMEM = pl.BlockSpec(memory_space=pltpu.VMEM)
SMEM = pl.BlockSpec(memory_space=pltpu.SMEM)
HBM = pl.BlockSpec(memory_space=pl.ANY)
LIMITS = {"conv_first": 60, "hop": 50}
PART = 512
SECTION = 128
TARGET, SOURCE, PLACE, ROUTE, OWN, OTHER, FROM, SPARE = (SECTION * i for i in range(8))
TABLE = 8 * SECTION
COUNT = TABLE - 1
GROUP = 8


def dot(a, b):
    return jnp.dot(a, b, preferred_element_type=F32)


def call(kernel, name, ins, outs, in_specs, out_specs, flops, scratch=(), alias=None):
    moved = sum(x.size * x.dtype.itemsize for x in ins) + sum(
        o.size * o.dtype.itemsize for o in outs
    )
    return pl.pallas_call(
        kernel,
        name=name,
        out_shape=tuple(outs),
        in_specs=in_specs,
        out_specs=tuple(out_specs),
        scratch_shapes=scratch,
        input_output_aliases=alias or {},
        compiler_params=pltpu.CompilerParams(vmem_limit_bytes=LIMITS.get(name, 52) << 20),
        cost_estimate=pl.CostEstimate(flops=flops, bytes_accessed=moved, transcendentals=0),
    )(*ins)


def shape(dims, dtype):
    return jax.ShapeDtypeStruct(dims, dtype)


def start(source, target, sem):
    copy = pltpu.make_async_copy(source, target, sem)
    copy.start()
    return copy


def tile_copy(field, tile, send, place, sem):
    rows = pl.ds(pl.multiple_of(tile * TILE, TILE), TILE)
    return pltpu.make_async_copy(field.at[rows, :], send.at[place], sem)


class Sends:
    def __init__(self, table, field, send, sems):
        self.groups = []
        count = table[COUNT]
        for g in range(send.shape[0] // GROUP):
            live = count > g * GROUP

            @pl.when(live)
            def _():
                for i in range(g * GROUP, (g + 1) * GROUP):
                    tile_copy(field, table[ROUTE + i], send, table[PLACE + i], sems.at[g]).start()

            some = send.at[pl.ds(0, GROUP)]
            self.groups.append((live, pltpu.make_async_copy(some, some, sems.at[g])))

    def wait(self):
        for live, copy in self.groups:
            pl.when(live)(copy.wait)


def start_sends(tile_of, field, send, sem):
    for place in range(send.shape[0]):
        tile_copy(field, tile_of(place), send, place, sem).start()
    return pltpu.make_async_copy(send, send, sem)


def start_parts(source, target, sem, parts):
    step = source.shape[0] // parts
    for i in range(parts):
        at = pl.ds(i * step, step)
        start(source.at[at, :], target.at[at, :], sem)
    return pltpu.make_async_copy(source, target, sem)


def start_far(table, far, near, sem):
    for j in range(near.shape[0]):
        start(far.at[table[SOURCE + j]], near.at[j], sem)
    return pltpu.make_async_copy(near, near, sem)


def add_arrived(table, blocks, far, total):
    for j in range(blocks.shape[0]):
        rows = pl.ds(pl.multiple_of(table[TARGET + j] * TILE, TILE), TILE)
        total[rows, :] += dot(blocks[j], far[table[SOURCE + j]])


def add_remote(table, blocks, near, total):
    for j in range(blocks.shape[0]):
        rows = pl.ds(pl.multiple_of(table[TARGET + j] * TILE, TILE), TILE)
        total[rows, :] += dot(blocks[j], near[j])


def convolve(past, state, weight, bias, gated, gated_out, sem, ready=None):
    gate = gated.shape[1]
    for i in range(state.shape[0] // PART):
        at = pl.ds(i * PART, PART)
        if ready is not None:
            ready(i)
        both = jnp.concatenate([past[at, :], state[at, :]], axis=1)
        pre = dot(both, weight[...]) + bias[...]
        value = jnp.tanh(pre[:, :gate]) * (0.5 * jnp.tanh(0.5 * pre[:, gate:]) + 0.5)
        gated[at, :] = value.astype(BF16)
        start(gated.at[at, :], gated_out.at[at, :], sem)
    return pltpu.make_async_copy(gated, gated_out, sem)


def weight_loads(layer, weight_all, bias_all, mix_all, weight, bias, mix, sems):
    depth = mix.shape[0]
    return [
        start(weight_all.at[layer], weight, sems.at[0]),
        start(bias_all.at[pl.ds(layer, 1), :], bias, sems.at[1]),
        start(mix_all.at[layer, pl.ds(2 * depth, depth), :], mix, sems.at[2]),
    ]


def first_kernel(
    tiles_in, state_in, past_all, weight_all, bias_all, mix_all,
    gated_out, send,
    past, weight, bias, mix, gated, second, state, tiles, sems, parts, *, layer,
):
    loads = weight_loads(layer, weight_all, bias_all, mix_all, weight, bias, mix, sems)
    pieces = []
    for i in range(state.shape[0] // PART):
        at = pl.ds(i * PART, PART)
        pieces.append(
            (
                start(past_all.at[layer, at, :], past.at[at, :], parts.at[2 * i]),
                start(state_in.at[at, :], state.at[at, :], parts.at[2 * i + 1]),
            )
        )
    routes = start(tiles_in, tiles, sems.at[4])

    def ready(i):
        if i == 0:
            for copy in loads:
                copy.wait()
        for copy in pieces[i]:
            copy.wait()

    copies = [convolve(past, state, weight, bias, gated, gated_out, sems.at[3], ready)]
    second[...] = dot(gated[...], mix[...]).astype(BF16)
    routes.wait()
    def tile_of(place):
        peer, slot = divmod(place, CAP)
        return tiles[0, slot, peer]

    copies.append(start_sends(tile_of, second, send, sems.at[5]))
    for copy in copies:
        copy.wait()


def receive(table_in, part_in, table, part, total, sems, more=lambda: None, far=None, near=None):
    waits = [start(table_in, table, sems.at[0])]
    if near is not None:
        waits.append(start_parts(far, near, sems.at[2], 4))
    if part is not None:
        waits.append(start_parts(part_in, part, sems.at[1], 1))
    total[...] = jnp.zeros_like(total)
    result = more()
    for copy in waits:
        copy.wait()
    return result


def joined(part, total):
    return (part.astype(F32) + total).astype(BF16)


def next_kernel(
    table_in, blocks, far, part_in, past_all, weight_all, bias_all, mix_all,
    gated_out, send,
    past, weight, bias, mix, gated, second, state, table, part, total, near, arrive, sems, send_sems,
    *, layer,
):
    def more():
        loads = weight_loads(layer, weight_all, bias_all, mix_all, weight, bias, mix, sems)
        loads.append(start_parts(past_all.at[layer], past, sems.at[4], 1))
        return loads

    loads = receive(table_in, part_in, table, part, total, arrive, more, far, near)
    add_arrived(table, blocks, near, total)
    state[...] = joined(part[...], total[...])
    for copy in loads:
        copy.wait()
    copies = [convolve(past, state, weight, bias, gated, gated_out, sems.at[3])]
    second[...] = dot(gated[...], mix[...]).astype(BF16)
    copies.append(Sends(table, second, send, send_sems))
    for copy in copies:
        copy.wait()


def hop_kernel(
    table_in, blocks, far, part_in, send, field, table, total, arrive, send_sems
):
    receive(table_in, part_in, table, None, total, arrive)
    add_arrived(table, blocks, far, total)
    field[...] = joined(part_in[...], total[...])
    Sends(table, field, send, send_sems).wait()


def last_kernel(
    table_in, blocks, far, part_in, state_out, state, table, part, total, near, arrive, sem
):
    receive(table_in, part_in, table, part, total, arrive, far=far, near=near)
    add_arrived(table, blocks, near, total)
    state[...] = joined(part[...], total[...])
    start_parts(state, state_out, sem.at[0], 2).wait()


def build_kernel(place, target, owner, slot, tiles, count, values, table, remote_blocks):
    me = place[0]

    def body(b, seen):
        t, o, s = target[b], owner[b], slot[b]
        mine = o == me

        @pl.when(mine)
        def _():
            table[jnp.where(s == t, OWN, OTHER) + t] = b
            table[jnp.where(s == t, SPARE, FROM) + t] = s

        @pl.when(jnp.logical_not(mine))
        def _():
            table[TARGET + seen] = t
            table[SOURCE + seen] = o * CAP + s
            remote_blocks[seen] = values[b]

        return seen + jnp.where(mine, 0, 1)

    lax.fori_loop(0, target.shape[0], body, jnp.int32(0))
    slots = tiles.shape[2] * CAP
    live = dead = jnp.int32(0)
    for peer in range(tiles.shape[2]):
        for s in range(CAP):
            used = count[0, peer] > s
            at = jnp.where(used, live, slots - 1 - dead)
            table[PLACE + at] = peer * CAP + s
            table[ROUTE + at] = tiles[0, s, peer]
            live = live + jnp.where(used, 1, 0)
            dead = dead + jnp.where(used, 0, 1)
    table[COUNT] = live


def local_sum(table, values, field, t):
    other = field[pl.ds(pl.multiple_of(table[FROM + t] * TILE, TILE), TILE), :]
    own = field[pl.ds(t * TILE, TILE), :]
    block = jnp.concatenate([values[table[OWN + t]], values[table[OTHER + t]]], axis=1)
    return dot(block, jnp.concatenate([own, other], axis=0))


def under_first_kernel(table, values, gated, mix_all, skip_all, *rest, res, layer):
    if layer:
        skip_in, blocks, far, part_in, *rest = rest
    else:
        state, *rest = rest
    total, base, skip, wide, deep, second, sems = rest[:7]
    gate = gated.shape[1]
    loads = [
        start(mix_all.at[layer, pl.ds(2 * gate, gate), :], deep, sems.at[3]),
        start(mix_all.at[layer, pl.ds(gate, gate), :], wide.at[:, pl.ds(0, res)], sems.at[0]),
        start(mix_all.at[layer, pl.ds(0, gate), :], wide.at[:, pl.ds(res, res)], sems.at[1]),
        start(skip_all.at[layer], wide.at[:, pl.ds(2 * res, skip.shape[1])], sems.at[2]),
    ]
    if layer:
        near, part, sums = rest[7:]
        loads.append(start_far(table, far, near, sems.at[4]))
        loads.append(start_parts(part_in, part, sems.at[5], 4))
        sums[...] = jnp.zeros_like(sums)
    for copy in loads:
        copy.wait()
    if layer:
        add_remote(table, blocks, near, sums)
    second[...] = dot(gated[...], deep[...]).astype(BF16)
    for t in range(gated.shape[0] // TILE):
        at = pl.ds(t * TILE, TILE)
        out = dot(gated[at, :], wide[...])
        total[at, :] = (out[:, :res] + local_sum(table, values, second, t)).astype(BF16)
        now = joined(part[at, :], sums[at, :]) if layer else state[at, :]
        base[at, :] = now.astype(F32) + out[:, res : 2 * res]
        gain = out[:, 2 * res :]
        if layer:
            gain = gain + skip_in[at, :]
        skip[at, :] = gain.astype(skip.dtype)


def under_second_kernel(
    table, values, blocks, far, part_in, base, part_out, field, near, part, total, sems
):
    loads = [
        start_far(table, far, near, sems.at[0]),
        start_parts(part_in, part, sems.at[1], 4),
    ]
    total[...] = jnp.zeros_like(total)
    for copy in loads:
        copy.wait()
    add_remote(table, blocks, near, total)
    field[...] = joined(part[...], total[...])
    for t in range(field.shape[0] // TILE):
        at = pl.ds(t * TILE, TILE)
        part_out[at, :] = (base[at, :] + local_sum(table, values, field, t)).astype(BF16)


def local(
    hidden_state,
    conv_cache,
    conv_weight,
    conv_bias,
    mix_weight,
    skip_weight,
    block_values,
    block_target,
    block_owner,
    block_slot,
    send_tiles,
    send_count,
):
    rows, res = hidden_state.shape
    layers = conv_cache.shape[0]
    gate, skips = skip_weight.shape[1:]
    tiles = rows // TILE
    peers = send_tiles.shape[1]
    slots = peers * CAP
    send_tiles = jnp.swapaxes(send_tiles, 1, 2)
    blocks = block_values.shape[0]
    remote = blocks - 2 * tiles
    place = lax.axis_index("node").astype(jnp.int32)[None]
    assert max(slots, remote, tiles) <= SECTION

    table, remote_blocks = call(
        build_kernel,
        "sort_blocks",
        (place, block_target, block_owner, block_slot, send_tiles, send_count, block_values),
        (shape((TABLE,), jnp.int32), shape((remote, TILE, TILE), BF16)),
        [SMEM] * 6 + [VMEM],
        [SMEM, VMEM],
        blocks * 1000,
    )

    def exchange(send):
        got = lax.all_to_all(
            send.reshape(peers, CAP, TILE, res), "node", split_axis=0, concat_axis=0, tiled=True
        )
        return got.reshape(slots, TILE, res)

    conv_flops = 2 * rows * (2 * res * 2 * gate + gate * res)
    hop_flops = 2 * remote * TILE * TILE * res
    conv_outs = (shape((rows, gate), BF16), shape((slots, TILE, res), BF16))
    conv_scratch = [
        pltpu.VMEM((rows, res), BF16),
        pltpu.VMEM((2 * res, 2 * gate), BF16),
        pltpu.VMEM((1, 2 * gate), F32),
        pltpu.VMEM((gate, res), BF16),
        pltpu.VMEM((rows, gate), BF16),
        pltpu.VMEM((rows, res), BF16),
        pltpu.VMEM((rows, res), BF16),
    ]
    near = pltpu.VMEM((remote, TILE, res), BF16)
    wide_field = pltpu.VMEM((rows, res), F32)
    thin_field = pltpu.VMEM((rows, res), BF16)
    index = pltpu.SMEM((TABLE,), jnp.int32)

    def sems(n):
        return pltpu.SemaphoreType.DMA((n,))

    arrival = [index, thin_field, wide_field, pltpu.VMEM((slots, TILE, res), BF16), sems(3)]
    direct_arrival = [index, wide_field, sems(1)]
    weights = (conv_cache, conv_weight, conv_bias, mix_weight)
    state = hidden_state
    skip = None
    total = far = None
    for layer in range(layers):
        if layer == 0:
            gated, send = call(
                functools.partial(first_kernel, layer=layer),
                "conv_first",
                (send_tiles, state) + weights,
                conv_outs,
                [HBM] * 6,
                [HBM] * 2,
                conv_flops,
                conv_scratch
                + [
                    pltpu.SMEM(send_tiles.shape, jnp.int32),
                    sems(6),
                    sems(2 * rows // PART),
                ],
            )
        else:
            gated, send = call(
                functools.partial(next_kernel, layer=layer),
                "conv_next",
                (table, remote_blocks, far, total) + weights,
                conv_outs,
                [HBM, VMEM] + [HBM] * 6,
                [HBM] * 2,
                conv_flops + hop_flops,
                conv_scratch + arrival + [sems(6), sems(slots // GROUP)],
            )
        old_far, old_total, far = far, total, exchange(send)
        last = layer == layers - 1
        ins = (table, block_values, gated, mix_weight, skip_weight)
        ins += (skip, remote_blocks, old_far, old_total) if layer else (hidden_state,)
        total, base, skip = call(
            functools.partial(under_first_kernel, res=res, layer=layer),
            "under_first",
            ins,
            (
                shape((rows, res), BF16),
                shape((rows, res), F32),
                shape((rows, skips), BF16 if last else F32),
            ),
            [SMEM] + [VMEM] * 2 + [HBM] * 2 + ([VMEM] * 2 + [HBM] * 2 if layer else [VMEM]),
            [VMEM] * 3,
            2 * rows * gate * (3 * res + skips) + 4 * rows * TILE * res,
            [
                pltpu.VMEM((gate, 2 * res + skips), BF16),
                pltpu.VMEM((gate, res), BF16),
                thin_field,
                sems(6),
            ]
            + ([near, thin_field, wide_field] if layer else []),
        )
        (send,) = call(
            hop_kernel,
            "hop",
            (table, remote_blocks, far, total),
            (shape((slots, TILE, res), BF16),),
            [HBM, VMEM, VMEM, VMEM],
            [HBM],
            hop_flops,
            [thin_field] + direct_arrival + [sems(slots // GROUP)],
        )
        near_far, far = far, exchange(send)
        (total,) = call(
            under_second_kernel,
            "under_second",
            (table, block_values, remote_blocks, near_far, total, base),
            (shape((rows, res), BF16),),
            [SMEM] + [VMEM] * 2 + [HBM] * 2 + [VMEM],
            [VMEM],
            4 * rows * TILE * res + hop_flops,
            [thin_field, near, thin_field, wide_field, sems(2)],
        )
    (state,) = call(
        last_kernel,
        "last",
        (table, remote_blocks, far, total),
        (shape((rows, res), BF16),),
        [HBM, VMEM, HBM, HBM],
        [HBM],
        hop_flops,
        [thin_field] + arrival + [sems(1)],
    )
    return state, skip


def solution(mesh):
    placed = (
        P(("scen", "node"), None),
        P(None, ("scen", "node"), None),
        P(),
        P(),
        P(),
        P(),
        P("node", None, None),
        P("node"),
        P("node"),
        P("node"),
        P("node", None, None),
        P("node", None),
    )
    return jax.shard_map(
        local,
        mesh=mesh,
        in_specs=placed,
        out_specs=(P(("scen", "node"), None), P(("scen", "node"), None)),
        check_vma=False,
    )
```

```python
import functools

import jax
import jax.numpy as jnp
from jax import lax
from jax.experimental import pallas as pl
from jax.experimental.pallas import tpu as pltpu
from jax.sharding import PartitionSpec as P

TILE = 128
CAP = 2
F32 = jnp.float32
BF16 = jnp.bfloat16
VMEM = pl.BlockSpec(memory_space=pltpu.VMEM)
SMEM = pl.BlockSpec(memory_space=pltpu.SMEM)
HBM = pl.BlockSpec(memory_space=pl.ANY)
LIMITS = {"conv_first": 60, "hop": 50}
PART = 512
SECTION = 128
TARGET, SOURCE, PLACE, ROUTE, OWN, OTHER, FROM, SPARE = (SECTION * i for i in range(8))
TABLE = 8 * SECTION
COUNT = TABLE - 1
GROUP = 8


def dot(a, b):
    return jnp.dot(a, b, preferred_element_type=F32)


def call(kernel, name, ins, outs, in_specs, out_specs, flops, scratch=(), alias=None):
    moved = sum(x.size * x.dtype.itemsize for x in ins) + sum(
        o.size * o.dtype.itemsize for o in outs
    )
    return pl.pallas_call(
        kernel,
        name=name,
        out_shape=tuple(outs),
        in_specs=in_specs,
        out_specs=tuple(out_specs),
        scratch_shapes=scratch,
        input_output_aliases=alias or {},
        compiler_params=pltpu.CompilerParams(vmem_limit_bytes=LIMITS.get(name, 52) << 20),
        cost_estimate=pl.CostEstimate(flops=flops, bytes_accessed=moved, transcendentals=0),
    )(*ins)


def shape(dims, dtype):
    return jax.ShapeDtypeStruct(dims, dtype)


def start(source, target, sem):
    copy = pltpu.make_async_copy(source, target, sem)
    copy.start()
    return copy


def tile_copy(field, tile, send, place, sem):
    rows = pl.ds(pl.multiple_of(tile * TILE, TILE), TILE)
    return pltpu.make_async_copy(field.at[rows, :], send.at[place], sem)


class Sends:
    def __init__(self, table, field, send, sems):
        self.groups = []
        count = table[COUNT]
        for g in range(send.shape[0] // GROUP):
            live = count > g * GROUP

            @pl.when(live)
            def _():
                for i in range(g * GROUP, (g + 1) * GROUP):
                    tile_copy(field, table[ROUTE + i], send, table[PLACE + i], sems.at[g]).start()

            some = send.at[pl.ds(0, GROUP)]
            self.groups.append((live, pltpu.make_async_copy(some, some, sems.at[g])))

    def wait(self):
        for live, copy in self.groups:
            pl.when(live)(copy.wait)


def start_sends(tile_of, field, send, sem):
    for place in range(send.shape[0]):
        tile_copy(field, tile_of(place), send, place, sem).start()
    return pltpu.make_async_copy(send, send, sem)


def start_parts(source, target, sem, parts):
    step = source.shape[0] // parts
    for i in range(parts):
        at = pl.ds(i * step, step)
        start(source.at[at, :], target.at[at, :], sem)
    return pltpu.make_async_copy(source, target, sem)


def start_far(table, far, near, sem):
    for j in range(near.shape[0]):
        start(far.at[table[SOURCE + j]], near.at[j], sem)
    return pltpu.make_async_copy(near, near, sem)


def add_arrived(table, blocks, far, total):
    for j in range(blocks.shape[0]):
        rows = pl.ds(pl.multiple_of(table[TARGET + j] * TILE, TILE), TILE)
        total[rows, :] += dot(blocks[j], far[table[SOURCE + j]])


def add_remote(table, blocks, near, total):
    for j in range(blocks.shape[0]):
        rows = pl.ds(pl.multiple_of(table[TARGET + j] * TILE, TILE), TILE)
        total[rows, :] += dot(blocks[j], near[j])


def convolve(past, state, weight, bias, gated, gated_out, sem, ready=None):
    gate = gated.shape[1]
    for i in range(state.shape[0] // PART):
        at = pl.ds(i * PART, PART)
        if ready is not None:
            ready(i)
        both = jnp.concatenate([past[at, :], state[at, :]], axis=1)
        pre = dot(both, weight[...]) + bias[...]
        value = jnp.tanh(pre[:, :gate]) * (0.5 * jnp.tanh(0.5 * pre[:, gate:]) + 0.5)
        gated[at, :] = value.astype(BF16)
        start(gated.at[at, :], gated_out.at[at, :], sem)
    return pltpu.make_async_copy(gated, gated_out, sem)


def weight_loads(layer, weight_all, bias_all, mix_all, weight, bias, mix, sems):
    depth = mix.shape[0]
    return [
        start(weight_all.at[layer], weight, sems.at[0]),
        start(bias_all.at[pl.ds(layer, 1), :], bias, sems.at[1]),
        start(mix_all.at[layer, pl.ds(2 * depth, depth), :], mix, sems.at[2]),
    ]


def first_kernel(
    tiles_in, state_in, past_all, weight_all, bias_all, mix_all,
    gated_out, send,
    past, weight, bias, mix, gated, second, state, tiles, sems, parts, *, layer,
):
    loads = weight_loads(layer, weight_all, bias_all, mix_all, weight, bias, mix, sems)
    pieces = []
    for i in range(state.shape[0] // PART):
        at = pl.ds(i * PART, PART)
        pieces.append(
            (
                start(past_all.at[layer, at, :], past.at[at, :], parts.at[2 * i]),
                start(state_in.at[at, :], state.at[at, :], parts.at[2 * i + 1]),
            )
        )
    routes = start(tiles_in, tiles, sems.at[4])

    def ready(i):
        if i == 0:
            for copy in loads[:2]:
                copy.wait()
        for copy in pieces[i]:
            copy.wait()

    copies = [convolve(past, state, weight, bias, gated, gated_out, sems.at[3], ready)]
    loads[2].wait()
    second[...] = dot(gated[...], mix[...]).astype(BF16)
    routes.wait()
    def tile_of(place):
        peer, slot = divmod(place, CAP)
        return tiles[0, slot, peer]

    copies.append(start_sends(tile_of, second, send, sems.at[5]))
    for copy in copies:
        copy.wait()


def receive(table_in, part_in, table, part, total, sems, more=lambda: None, far=None, near=None):
    waits = [start(table_in, table, sems.at[0])]
    if near is not None:
        waits.append(start_parts(far, near, sems.at[2], 4))
    if part is not None:
        waits.append(start_parts(part_in, part, sems.at[1], 1))
    total[...] = jnp.zeros_like(total)
    result = more()
    for copy in waits:
        copy.wait()
    return result


def joined(part, total):
    return (part.astype(F32) + total).astype(BF16)


def next_kernel(
    table_in, blocks, far, part_in, past_all, weight_all, bias_all, mix_all,
    gated_out, send,
    past, weight, bias, mix, gated, second, state, table, part, total, near, arrive, sems, send_sems,
    *, layer,
):
    def more():
        loads = weight_loads(layer, weight_all, bias_all, mix_all, weight, bias, mix, sems)
        loads.append(start_parts(past_all.at[layer], past, sems.at[4], 1))
        return loads

    loads = receive(table_in, part_in, table, part, total, arrive, more, far, near)
    add_arrived(table, blocks, near, total)
    state[...] = joined(part[...], total[...])
    for copy in loads[:2] + loads[3:]:
        copy.wait()
    copies = [convolve(past, state, weight, bias, gated, gated_out, sems.at[3])]
    loads[2].wait()
    second[...] = dot(gated[...], mix[...]).astype(BF16)
    copies.append(Sends(table, second, send, send_sems))
    for copy in copies:
        copy.wait()


def hop_kernel(
    table_in, blocks, far, part_in, send, field, table, total, arrive, send_sems
):
    receive(table_in, part_in, table, None, total, arrive)
    add_arrived(table, blocks, far, total)
    field[...] = joined(part_in[...], total[...])
    Sends(table, field, send, send_sems).wait()


def last_kernel(
    table_in, blocks, far, part_in, state_out, state, table, part, total, near, arrive, sem
):
    receive(table_in, part_in, table, part, total, arrive, far=far, near=near)
    add_arrived(table, blocks, near, total)
    state[...] = joined(part[...], total[...])
    start_parts(state, state_out, sem.at[0], 2).wait()


def build_kernel(place, target, owner, slot, tiles, count, values, table, remote_blocks):
    me = place[0]

    def body(b, seen):
        t, o, s = target[b], owner[b], slot[b]
        mine = o == me

        @pl.when(mine)
        def _():
            table[jnp.where(s == t, OWN, OTHER) + t] = b
            table[jnp.where(s == t, SPARE, FROM) + t] = s

        @pl.when(jnp.logical_not(mine))
        def _():
            table[TARGET + seen] = t
            table[SOURCE + seen] = o * CAP + s
            remote_blocks[seen] = values[b]

        return seen + jnp.where(mine, 0, 1)

    lax.fori_loop(0, target.shape[0], body, jnp.int32(0))
    slots = tiles.shape[2] * CAP
    live = dead = jnp.int32(0)
    for peer in range(tiles.shape[2]):
        for s in range(CAP):
            used = count[0, peer] > s
            at = jnp.where(used, live, slots - 1 - dead)
            table[PLACE + at] = peer * CAP + s
            table[ROUTE + at] = tiles[0, s, peer]
            live = live + jnp.where(used, 1, 0)
            dead = dead + jnp.where(used, 0, 1)
    table[COUNT] = live


def local_sum(table, values, field, t):
    other = field[pl.ds(pl.multiple_of(table[FROM + t] * TILE, TILE), TILE), :]
    own = field[pl.ds(t * TILE, TILE), :]
    block = jnp.concatenate([values[table[OWN + t]], values[table[OTHER + t]]], axis=1)
    return dot(block, jnp.concatenate([own, other], axis=0))


def under_first_kernel(table, values, gated, mix_all, skip_all, *rest, res, layer):
    if layer:
        skip_in, blocks, far, part_in, *rest = rest
    else:
        state, *rest = rest
    total, base, skip, wide, deep, second, sems = rest[:7]
    gate = gated.shape[1]
    loads = [
        start(mix_all.at[layer, pl.ds(2 * gate, gate), :], deep, sems.at[3]),
        start(mix_all.at[layer, pl.ds(gate, gate), :], wide.at[:, pl.ds(0, res)], sems.at[0]),
        start(mix_all.at[layer, pl.ds(0, gate), :], wide.at[:, pl.ds(res, res)], sems.at[1]),
        start(skip_all.at[layer], wide.at[:, pl.ds(2 * res, skip.shape[1])], sems.at[2]),
    ]
    if layer:
        near, part, sums = rest[7:]
        loads.append(start_far(table, far, near, sems.at[4]))
        loads.append(start_parts(part_in, part, sems.at[5], 4))
        sums[...] = jnp.zeros_like(sums)
    for copy in loads:
        copy.wait()
    if layer:
        add_remote(table, blocks, near, sums)
    second[...] = dot(gated[...], deep[...]).astype(BF16)
    for t in range(gated.shape[0] // TILE):
        at = pl.ds(t * TILE, TILE)
        out = dot(gated[at, :], wide[...])
        total[at, :] = (out[:, :res] + local_sum(table, values, second, t)).astype(BF16)
        now = joined(part[at, :], sums[at, :]) if layer else state[at, :]
        base[at, :] = now.astype(F32) + out[:, res : 2 * res]
        gain = out[:, 2 * res :]
        if layer:
            gain = gain + skip_in[at, :]
        skip[at, :] = gain.astype(skip.dtype)


def under_second_kernel(
    table, values, blocks, far, part_in, base, part_out, field, near, part, total, sems
):
    loads = [
        start_far(table, far, near, sems.at[0]),
        start_parts(part_in, part, sems.at[1], 4),
    ]
    total[...] = jnp.zeros_like(total)
    for copy in loads:
        copy.wait()
    add_remote(table, blocks, near, total)
    field[...] = joined(part[...], total[...])
    for t in range(field.shape[0] // TILE):
        at = pl.ds(t * TILE, TILE)
        part_out[at, :] = (base[at, :] + local_sum(table, values, field, t)).astype(BF16)


def local(
    hidden_state,
    conv_cache,
    conv_weight,
    conv_bias,
    mix_weight,
    skip_weight,
    block_values,
    block_target,
    block_owner,
    block_slot,
    send_tiles,
    send_count,
):
    rows, res = hidden_state.shape
    layers = conv_cache.shape[0]
    gate, skips = skip_weight.shape[1:]
    tiles = rows // TILE
    peers = send_tiles.shape[1]
    slots = peers * CAP
    send_tiles = jnp.swapaxes(send_tiles, 1, 2)
    blocks = block_values.shape[0]
    remote = blocks - 2 * tiles
    place = lax.axis_index("node").astype(jnp.int32)[None]
    assert max(slots, remote, tiles) <= SECTION

    table, remote_blocks = call(
        build_kernel,
        "sort_blocks",
        (place, block_target, block_owner, block_slot, send_tiles, send_count, block_values),
        (shape((TABLE,), jnp.int32), shape((remote, TILE, TILE), BF16)),
        [SMEM] * 6 + [VMEM],
        [SMEM, VMEM],
        blocks * 1000,
    )

    def exchange(send):
        got = lax.all_to_all(
            send.reshape(peers, CAP, TILE, res), "node", split_axis=0, concat_axis=0, tiled=True
        )
        return got.reshape(slots, TILE, res)

    conv_flops = 2 * rows * (2 * res * 2 * gate + gate * res)
    hop_flops = 2 * remote * TILE * TILE * res
    conv_outs = (shape((rows, gate), BF16), shape((slots, TILE, res), BF16))
    conv_scratch = [
        pltpu.VMEM((rows, res), BF16),
        pltpu.VMEM((2 * res, 2 * gate), BF16),
        pltpu.VMEM((1, 2 * gate), F32),
        pltpu.VMEM((gate, res), BF16),
        pltpu.VMEM((rows, gate), BF16),
        pltpu.VMEM((rows, res), BF16),
        pltpu.VMEM((rows, res), BF16),
    ]
    near = pltpu.VMEM((remote, TILE, res), BF16)
    wide_field = pltpu.VMEM((rows, res), F32)
    thin_field = pltpu.VMEM((rows, res), BF16)
    index = pltpu.SMEM((TABLE,), jnp.int32)

    def sems(n):
        return pltpu.SemaphoreType.DMA((n,))

    arrival = [index, thin_field, wide_field, pltpu.VMEM((slots, TILE, res), BF16), sems(3)]
    direct_arrival = [index, wide_field, sems(1)]
    weights = (conv_cache, conv_weight, conv_bias, mix_weight)
    state = hidden_state
    skip = None
    total = far = None
    for layer in range(layers):
        if layer == 0:
            gated, send = call(
                functools.partial(first_kernel, layer=layer),
                "conv_first",
                (send_tiles, state) + weights,
                conv_outs,
                [HBM] * 6,
                [HBM] * 2,
                conv_flops,
                conv_scratch
                + [
                    pltpu.SMEM(send_tiles.shape, jnp.int32),
                    sems(6),
                    sems(2 * rows // PART),
                ],
            )
        else:
            gated, send = call(
                functools.partial(next_kernel, layer=layer),
                "conv_next",
                (table, remote_blocks, far, total) + weights,
                conv_outs,
                [HBM, VMEM] + [HBM] * 6,
                [HBM] * 2,
                conv_flops + hop_flops,
                conv_scratch + arrival + [sems(6), sems(slots // GROUP)],
            )
        old_far, old_total, far = far, total, exchange(send)
        last = layer == layers - 1
        ins = (table, block_values, gated, mix_weight, skip_weight)
        ins += (skip, remote_blocks, old_far, old_total) if layer else (hidden_state,)
        total, base, skip = call(
            functools.partial(under_first_kernel, res=res, layer=layer),
            "under_first",
            ins,
            (
                shape((rows, res), BF16),
                shape((rows, res), F32),
                shape((rows, skips), BF16 if last else F32),
            ),
            [SMEM] + [VMEM] * 2 + [HBM] * 2 + ([VMEM] * 2 + [HBM] * 2 if layer else [VMEM]),
            [VMEM] * 3,
            2 * rows * gate * (3 * res + skips) + 4 * rows * TILE * res,
            [
                pltpu.VMEM((gate, 2 * res + skips), BF16),
                pltpu.VMEM((gate, res), BF16),
                thin_field,
                sems(6),
            ]
            + ([near, thin_field, wide_field] if layer else []),
        )
        (send,) = call(
            hop_kernel,
            "hop",
            (table, remote_blocks, far, total),
            (shape((slots, TILE, res), BF16),),
            [HBM, VMEM, VMEM, VMEM],
            [HBM],
            hop_flops,
            [thin_field] + direct_arrival + [sems(slots // GROUP)],
        )
        near_far, far = far, exchange(send)
        (total,) = call(
            under_second_kernel,
            "under_second",
            (table, block_values, remote_blocks, near_far, total, base),
            (shape((rows, res), BF16),),
            [SMEM] + [VMEM] * 2 + [HBM] * 2 + [VMEM],
            [VMEM],
            4 * rows * TILE * res + hop_flops,
            [thin_field, near, thin_field, wide_field, sems(2)],
        )
    (state,) = call(
        last_kernel,
        "last",
        (table, remote_blocks, far, total),
        (shape((rows, res), BF16),),
        [HBM, VMEM, HBM, HBM],
        [HBM],
        hop_flops,
        [thin_field] + arrival + [sems(1)],
    )
    return state, skip


def solution(mesh):
    placed = (
        P(("scen", "node"), None),
        P(None, ("scen", "node"), None),
        P(),
        P(),
        P(),
        P(),
        P("node", None, None),
        P("node"),
        P("node"),
        P("node"),
        P("node", None, None),
        P("node", None),
    )
    return jax.shard_map(
        local,
        mesh=mesh,
        in_specs=placed,
        out_specs=(P(("scen", "node"), None), P(("scen", "node"), None)),
        check_vma=False,
    )
```
